32 devices in a mesh: batch: 8 (over z, core), proto: 4 (over y, x).
Axes of the slice: x: 2, y: 2, z: 4, core: 2. Of those that a mesh axis runs over, the one named last changes fastest.
Arguments:
- student_features: bfloat16 [10, 1024, 256], P(None, 'batch'), may hold values from -8 to 8
- teacher_features: bfloat16 [2, 1024, 256], P(None, 'batch'), may hold values from -8 to 8
- student_prototypes: bfloat16 [256, 65536], P(None, 'proto'), may hold values from -0.5 to 0.5
- teacher_prototypes: bfloat16 [256, 65536], P(None, 'proto'), may hold values from -0.5 to 0.5
Outputs:
- mean_loss: float32 [], replicated
- grad_features: float32 [10, 1024, 256], P(None, ('batch', 'proto'))
- grad_prototypes: float32 [256, 65536], P('batch', 'proto')
The draws below stay inside these ranges and needn't reach their ends.
All inputs are finite; a program needn't handle non-finite values.
Results may differ from the reference program's by a relative error of at most 0.001.
The reference program's roundings to bfloat16 on the way (of `student_bf`, `proto_bf` and `grad_cos`) count: a program that leaves them out, or rounds other values in their place, can miss the bound.
Values sent between devices are 32-bit elements; how exact they have to be, the bound alone decides.
No kernel may reach another device: no remote copies, remote signals or barrier semaphores. Data moves between devices by JAX's collectives and lax.ppermute only.
A program may use at most 512 MiB of HBM per device.

```python
import math
import jax
import jax.numpy as jnp
from jax import lax

D = 256
CLUSTER_NUMBER = 65536
CROPS = 10
WIDE_CROP_NUMBER = 2
SK_ITERS = 3
PICTURE_NUMBER = 1024
PAIRS = 18


def shared_parts(key):
    centers = jax.random.normal(jax.random.fold_in(key, 11), (8, D), jnp.float32)
    mixing = jax.random.normal(jax.random.fold_in(key, 13), (PICTURE_NUMBER, 8), jnp.float32)
    latent = jnp.dot(mixing, centers) / math.sqrt(8.0)
    labels = jax.random.randint(jax.random.fold_in(key, 17), (CLUSTER_NUMBER,), 0, 8)
    return (centers, latent, labels)


def crop_noise(key, shape):
    return jax.random.normal(key, shape, jnp.float32)


def draw_student_features(key, part):
    centers, latent, labels = shared_parts(key)
    noise = crop_noise(jax.random.fold_in(key, 21), (CROPS, PICTURE_NUMBER, D))
    values = 0.8 * latent[None] + 0.6 * noise
    return jnp.clip(values, -8.0, 8.0).astype(jnp.bfloat16)


def draw_teacher_features(key, part):
    centers, latent, labels = shared_parts(key)
    noise = crop_noise(jax.random.fold_in(key, 23), (WIDE_CROP_NUMBER, PICTURE_NUMBER, D))
    values = 0.9 * latent[None] + 0.45 * noise
    return jnp.clip(values, -8.0, 8.0).astype(jnp.bfloat16)


def proto_base(key):
    centers, latent, labels = shared_parts(key)
    noise = crop_noise(jax.random.fold_in(key, 31), (D, CLUSTER_NUMBER))
    return (0.7 * centers[labels].T + 0.7 * noise) / 16.0


def draw_student_prototypes(key, part):
    return jnp.clip(proto_base(key), -0.5, 0.5).astype(jnp.bfloat16)


def draw_teacher_prototypes(key, part):
    moved = proto_base(key) + 0.25 * jax.random.normal(jax.random.fold_in(key, 29), (D, CLUSTER_NUMBER), jnp.float32) / 16.0
    return jnp.clip(moved, -0.5, 0.5).astype(jnp.bfloat16)


def setup_inputs(seed: int = 0) -> dict:
    splits = jax.random.split(jax.random.key(seed), 5)
    return {
        "student_features": draw_student_features(jax.random.fold_in(splits[4], 71), 0),
        "teacher_features": draw_teacher_features(jax.random.fold_in(splits[4], 71), 0),
        "student_prototypes": draw_student_prototypes(jax.random.fold_in(splits[4], 71), 0),
        "teacher_prototypes": draw_teacher_prototypes(jax.random.fold_in(splits[4], 71), 0),
    }


STUDENT_TEMP = 0.1
TEACHER_TEMP = 0.07
NORM_EPS = 1e-06

def unit_rows(values):
    floats = values.astype(jnp.float32)
    inverse = lax.rsqrt(lax.optimization_barrier(jnp.sum(floats * floats, axis=-1, keepdims=True)) + NORM_EPS)
    return (floats * inverse, inverse)

def unit_columns(values):
    floats = values.astype(jnp.float32)
    inverse = lax.rsqrt(lax.optimization_barrier(jnp.sum(floats * floats, axis=0, keepdims=True)) + NORM_EPS)
    return (floats * inverse, inverse)

def equipartition_normalize(cluster_share, sample_number):
    for sweep_index in range(SK_ITERS):
        cluster_share = cluster_share / (CLUSTER_NUMBER * lax.optimization_barrier(jnp.sum(cluster_share, axis=0, keepdims=True)))
        cluster_share = cluster_share / (sample_number * lax.optimization_barrier(jnp.sum(cluster_share, axis=1, keepdims=True)))
    return sample_number * cluster_share

def reference(student_features, teacher_features, student_prototypes, teacher_prototypes):
    unit_student, student_scale = unit_rows(student_features)
    student_bf = unit_student.astype(jnp.bfloat16)
    unit_proto, proto_scale = unit_columns(student_prototypes)
    proto_bf = unit_proto.astype(jnp.bfloat16)
    unit_teacher, unused_scale = unit_rows(teacher_features)
    teacher_bf = unit_teacher.astype(jnp.bfloat16).reshape(WIDE_CROP_NUMBER * PICTURE_NUMBER, D)
    unit_tproto, unused_tscale = unit_columns(teacher_prototypes)
    teacher_proto_bf = unit_tproto.astype(jnp.bfloat16)
    mentor_logit_matrix = jnp.dot(teacher_bf, teacher_proto_bf, preferred_element_type=jnp.float32) / TEACHER_TEMP
    cluster_targets_matrix = equipartition_normalize(jnp.exp(mentor_logit_matrix), WIDE_CROP_NUMBER * PICTURE_NUMBER).reshape(WIDE_CROP_NUMBER, PICTURE_NUMBER, CLUSTER_NUMBER)
    first_global = cluster_targets_matrix[0]
    second_global = cluster_targets_matrix[1]
    summed = first_global + second_global
    factor = 1.0 / (PICTURE_NUMBER * PAIRS * STUDENT_TEMP)

    def crop_step(carried, inputs):
        weight_cot, curvature, loss_sum = carried
        crop_rows, crop_index = inputs
        logits = jnp.dot(crop_rows, proto_bf, preferred_element_type=jnp.float32) / STUDENT_TEMP
        log_norm = jnp.log(lax.optimization_barrier(jnp.sum(jnp.exp(logits), axis=1, keepdims=True)))
        targets = jnp.where(crop_index == 0, second_global, jnp.where(crop_index == 1, first_global, summed))
        pair_count = jnp.where(crop_index < 2, jnp.float32(1.0), jnp.float32(2.0))
        loss_sum = loss_sum + jnp.sum(targets * (log_norm - logits))
        grad_cos = ((pair_count * jnp.exp(logits - log_norm) - targets) * factor).astype(jnp.bfloat16)
        feature_cot = lax.dot_general(grad_cos, proto_bf, (((1,), (1,)), ((), ())), preferred_element_type=jnp.float32)
        weight_cot = weight_cot + lax.dot_general(crop_rows, grad_cos, (((0,), (0,)), ((), ())), preferred_element_type=jnp.float32)
        curvature = curvature + lax.optimization_barrier(jnp.sum(logits * STUDENT_TEMP * grad_cos.astype(jnp.float32), axis=0))
        return ((weight_cot, curvature, loss_sum), feature_cot)
    start = (jnp.zeros((D, CLUSTER_NUMBER), jnp.float32), jnp.zeros((CLUSTER_NUMBER,), jnp.float32), jnp.zeros((), jnp.float32))
    (weight_cot, curvature, loss_sum), feature_cot = lax.scan(crop_step, start, (student_bf, jnp.arange(CROPS, dtype=jnp.int32)))
    mean_loss = loss_sum / (PICTURE_NUMBER * PAIRS)
    grad_features = student_scale * (feature_cot - unit_student * lax.optimization_barrier(jnp.sum(unit_student * feature_cot, axis=-1, keepdims=True)))
    grad_prototypes = proto_scale * (weight_cot - unit_proto * curvature[None, :])
    return (mean_loss, grad_features, grad_prototypes)
```

```python
import functools
import math

import jax
import jax.numpy as jnp
from jax import lax
from jax.experimental import pallas as pl
from jax.experimental.pallas import tpu as pltpu
from jax.sharding import PartitionSpec as P

CLUSTER_NUMBER = 65536
SK_ITERS = 3
PAIRS = 18

STUDENT_TEMP = 0.1
TEACHER_TEMP = 0.07
NORM_EPS = 1e-06
LOG2E = math.log2(math.e)

CHUNKS = 4
MIB = 1 << 20
F32 = jnp.float32
BF16 = jnp.bfloat16
WHOLE = pl.BlockSpec(memory_space=pltpu.VMEM)
SCALARS = pl.BlockSpec(memory_space=pltpu.SMEM)


def vmem(shape, dtype):
    return pltpu.VMEM(shape, dtype)


def params(limit):
    return pltpu.CompilerParams(vmem_limit_bytes=limit * MIB)


def swap(value, axis, bit):
    size = lax.axis_size(axis)
    return lax.ppermute(value, axis, [(i, i ^ (1 << bit)) for i in range(size)])


def bits_of(size):
    return size.bit_length() - 1


def unit_rows(values):
    floats = values.astype(F32)
    inverse = lax.rsqrt(jnp.sum(floats * floats, axis=-1, keepdims=True) + NORM_EPS)
    return (floats * inverse, inverse)


def column_scale(floats):
    return lax.rsqrt(jnp.sum(floats * floats, axis=0, keepdims=True) + NORM_EPS)


def rows_to_lanes(partial):
    return jnp.concatenate(
        [
            jnp.sum(partial[i : i + 128].T, axis=0, keepdims=True)
            for i in range(0, partial.shape[0], 128)
        ],
        axis=1,
    )


def lanes_to_rows(values, start):
    return jnp.broadcast_to(values[:, start : start + 128], (128, 128)).T


def row_sums(unit, protos, width):
    rows, dim = unit.shape
    columns = protos.shape[1]
    steps = columns // width

    def kernel(unit_ref, proto_ref, out_ref, rows_ref, sum_ref):
        step = pl.program_id(0)

        @pl.when(step == 0)
        def _():
            rows_ref[...] = unit_ref[...].astype(BF16)
            sum_ref[...] = jnp.zeros_like(sum_ref)

        floats = proto_ref[...].astype(F32)
        proto_bf = (floats * column_scale(floats)).astype(BF16)
        for start in range(0, rows, 256):
            cos = jnp.dot(rows_ref[start : start + 256], proto_bf, preferred_element_type=F32)
            mass = jnp.exp2(cos * (LOG2E / STUDENT_TEMP))
            total = mass[:, :128]
            for lane in range(128, width, 128):
                total = total + mass[:, lane : lane + 128]
            sum_ref[start : start + 256] += total

        @pl.when(step == steps - 1)
        def _():
            out_ref[...] = rows_to_lanes(sum_ref[...])

    return pl.pallas_call(
        kernel,
        grid=(steps,),
        in_specs=[
            pl.BlockSpec((rows, dim), lambda i: (0, 0)),
            pl.BlockSpec((dim, width), lambda i: (0, i)),
        ],
        out_specs=pl.BlockSpec((1, rows), lambda i: (0, 0)),
        out_shape=jax.ShapeDtypeStruct((1, rows), F32),
        scratch_shapes=[pltpu.VMEM((rows, dim), BF16), pltpu.VMEM((rows, 128), F32)],
        compiler_params=params(24),
        name="row_sums",
    )(unit, protos)


def teacher_mass(place, gathered, protos, columns, width):
    part_rows, dim = gathered[0].shape
    rows = part_rows * len(gathered)
    steps = columns // width

    def kernel(place_ref, *refs):
        parts = refs[: len(gathered)]
        proto_ref, mass_ref, sum_ref, rows_ref = refs[len(gathered) :]
        step = pl.program_id(0)

        @pl.when(step == 0)
        def _():
            for j, part in enumerate(parts):
                start = pl.multiple_of((place_ref[0] ^ j) * part_rows, part_rows)
                rows_ref[pl.ds(start, part_rows)] = part[...].astype(BF16)

        floats = proto_ref[...].astype(F32)
        proto_bf = (floats * column_scale(floats)).astype(BF16)
        at = pl.multiple_of(step * width, width)
        total = jnp.zeros((1, width), F32)
        for start in range(0, rows, 256):
            cos = jnp.dot(rows_ref[start : start + 256], proto_bf, preferred_element_type=F32)
            mass = jnp.exp2(cos * (LOG2E / TEACHER_TEMP))
            mass_ref[start : start + 256, pl.ds(at, width)] = mass
            total = total + jnp.sum(mass, axis=0, keepdims=True)
        sum_ref[...] = total

    return pl.pallas_call(
        kernel,
        grid_spec=pltpu.PrefetchScalarGridSpec(
            num_scalar_prefetch=1,
            grid=(steps,),
            in_specs=[pl.BlockSpec((part_rows, dim), lambda i, s: (0, 0)) for _ in gathered]
            + [pl.BlockSpec((dim, width), lambda i, s: (0, s[0] * steps + i))],
            out_specs=[WHOLE, pl.BlockSpec((1, width), lambda i, s: (0, i))],
            scratch_shapes=[pltpu.VMEM((rows, dim), BF16)],
        ),
        out_shape=[vmem((rows, columns), F32), jax.ShapeDtypeStruct((1, columns), F32)],
        compiler_params=params(20),
        name="teacher_mass",
    )(place, *gathered, protos)


def row_pass(column_parts, mass):
    rows, columns = mass.shape

    def kernel(a_ref, b_ref, mass_ref, out_ref):
        scale = 1.0 / (CLUSTER_NUMBER * (a_ref[...] + b_ref[...]))
        pieces = []
        for start in range(0, rows, 128):
            total = jnp.zeros((128, 128), F32)
            for lane in range(0, columns, 128):
                total = total + (
                    mass_ref[start : start + 128, lane : lane + 128] * scale[:, lane : lane + 128]
                )
            pieces.append(jnp.sum(total.T, axis=0, keepdims=True))
        out_ref[...] = jnp.concatenate(pieces, axis=1)

    return pl.pallas_call(
        kernel,
        in_specs=[WHOLE] * 3,
        out_specs=WHOLE,
        out_shape=jax.ShapeDtypeStruct((1, rows), F32),
        compiler_params=params(16),
        name="row_pass",
    )(*column_parts, mass)


def column_pass(row_parts, mass, sample_number):
    rows, columns = mass.shape

    def kernel(a_ref, b_ref, mass_ref, out_ref, scale_ref):
        scale = 1.0 / (sample_number * (a_ref[...] + b_ref[...]))
        for start in range(0, rows, 128):
            scale_ref[start : start + 128] = lanes_to_rows(scale, start)
        for lane in range(0, columns, 128):
            total = jnp.zeros((8, 128), F32)
            for start in range(0, rows, 128):
                term = mass_ref[start : start + 128, lane : lane + 128] * scale_ref[start : start + 128]
                total = total + jnp.sum(term.reshape(16, 8, 128), axis=0)
            out_ref[:, lane : lane + 128] = jnp.sum(total, axis=0, keepdims=True)

    return pl.pallas_call(
        kernel,
        in_specs=[WHOLE] * 3,
        out_specs=WHOLE,
        out_shape=jax.ShapeDtypeStruct((1, columns), F32),
        scratch_shapes=[pltpu.VMEM((rows, 128), F32)],
        compiler_params=params(16),
        name="column_pass",
    )(*row_parts, mass)


def gather_rows(place, own, core, far, far_core, crops, images):
    dim = own.shape[1]
    part_rows = crops * images
    pieces, _, piece_images, _ = far.shape
    rows = 4 * part_rows

    def kernel(place_ref, own_ref, core_ref, far_ref, far_core_ref, rows_ref, cols_ref, work_ref):
        def store(j, values):
            start = pl.multiple_of((place_ref[0] ^ j) * part_rows, part_rows)
            rows_ref[pl.ds(start, part_rows)] = values.astype(BF16)
            cols_ref[:, pl.ds(start, part_rows)] = values.T.astype(BF16)

        store(0, own_ref[...])
        store(1, core_ref[...])
        for j, ref in ((2, far_ref), (3, far_core_ref)):
            for piece in range(pieces):
                offset = (place_ref[1] ^ piece) * piece_images
                for crop in range(crops):
                    at = pl.multiple_of(crop * images + offset, piece_images)
                    work_ref[pl.ds(at, piece_images)] = ref[piece, crop]
            store(j, work_ref[...])

    return pl.pallas_call(
        kernel,
        in_specs=[SCALARS] + [WHOLE] * 4,
        out_specs=[WHOLE] * 2,
        out_shape=[vmem((rows, dim), BF16), vmem((dim, rows), BF16)],
        scratch_shapes=[pltpu.VMEM((part_rows, dim), F32)],
        compiler_params=params(24),
        name="gather_rows",
    )(place, own, core, far, far_core)


def row_offsets(sums, crops, images, factor):
    rows = sums.shape[1]

    def kernel(sums_ref, out_ref):
        for start in range(0, rows, 128):
            crop = (start // images) % crops
            pair_count = 1.0 if crop < 2 else 2.0
            values = jnp.log2((pair_count * factor) / sums_ref[:, start : start + 128])
            out_ref[start : start + 128] = lanes_to_rows(values, 0)

    return pl.pallas_call(
        kernel,
        in_specs=[WHOLE],
        out_specs=WHOLE,
        out_shape=vmem((rows, 128), F32),
        compiler_params=params(16),
        name="row_offsets",
    )(sums)


def gradients(place, chunk, chunks, protos, mass, column_sums, row_sum, rows, cols, offsets, carried, geometry, width):
    crops, images, pieces, blocks, factor, order = geometry
    dim = protos.shape[0]
    row_count = rows.shape[0]
    teacher_rows, columns = mass.shape
    groups = teacher_rows // (2 * images)
    part_rows = crops * images
    piece_images = images // pieces
    steps = columns // chunks // width
    total_steps = columns // width
    block_rows = dim // blocks
    first, last = chunk == 0, chunk == chunks - 1
    half = row_count // 2 // part_rows

    def kernel(place_ref, *refs):
        refs = list(refs)
        proto_ref, mass_ref, csum_ref, rsum_ref, rows_ref, cols_ref, offs_ref = refs[:7]
        refs = refs[7:]
        if not first:
            feat_in, targ_in = refs[:2]
            refs = refs[2:]
        send_ref, keep_ref = refs[:2]
        refs = refs[2:]
        if last:
            far_ref, near_ref, loss_ref = refs[:3]
            refs = refs[3:]
            if first:
                feat_ref, targ_ref = refs[:2]
                refs = refs[2:]
            else:
                feat_ref, targ_ref = feat_in, targ_in
        else:
            feat_ref, targ_ref = refs[:2]
            refs = refs[2:]
        grad_ref, tbf_ref, rscale_ref, weight_ref = refs
        step = pl.program_id(0)

        @pl.when(step == 0)
        def _():
            scale = factor / rsum_ref[...]
            for start in range(0, teacher_rows, 128):
                rscale_ref[start : start + 128] = lanes_to_rows(scale, start)
            if first:
                feat_ref[...] = jnp.zeros_like(feat_ref)
                targ_ref[...] = jnp.zeros_like(targ_ref)

        at = pl.multiple_of((chunk * steps + step) * width, width)
        floats = proto_ref[...].astype(F32)
        inverse = column_scale(floats)
        unit = floats * inverse
        proto_bf = unit.astype(BF16)
        proto_t = unit.T.astype(BF16)
        cscale = 1.0 / (CLUSTER_NUMBER * csum_ref[:, pl.ds(at, width)])

        for group in range(groups):
            base = group * part_rows
            tbase = group * 2 * images
            for image in range(0, images, 128):
                pair = []
                for wide in range(2):
                    start = tbase + wide * images + image
                    rscale = jnp.concatenate([rscale_ref[start : start + 128]] * (width // 128), axis=1)
                    target = mass_ref[start : start + 128, pl.ds(at, width)] * rscale * cscale
                    tbf_ref[start : start + 128] = target.astype(BF16)
                    pair.append(target)
                both = pair[0] + pair[1]
                for crop in range(crops):
                    start = base + crop * images + image
                    cos = jnp.dot(rows_ref[start : start + 128], proto_bf, preferred_element_type=F32)
                    offset = jnp.concatenate([offs_ref[start : start + 128]] * (width // 128), axis=1)
                    prob = jnp.exp2(cos * (LOG2E / STUDENT_TEMP) + offset)
                    target = pair[1] if crop == 0 else pair[0] if crop == 1 else both
                    grad_ref[start : start + 128] = (prob - target).astype(BF16)
            feat_ref[base : base + part_rows] += jnp.dot(
                grad_ref[base : base + part_rows], proto_t, preferred_element_type=F32
            )
        targ_ref[...] += jnp.dot(tbf_ref[...], proto_t, preferred_element_type=F32)
        weight = jnp.dot(cols_ref[...], grad_ref[...], preferred_element_type=F32)
        curvature = jnp.sum(proto_bf.astype(F32) * weight, axis=0, keepdims=True)
        weight_ref[...] = inverse * (weight - unit * curvature)
        for position, j in enumerate(order):
            start = pl.multiple_of((place_ref[1] ^ j) * block_rows, block_rows)
            dest, index = (keep_ref, position) if position < blocks // 2 else (send_ref, position - blocks // 2)
            dest[index * block_rows : (index + 1) * block_rows] = weight_ref[pl.ds(start, block_rows)]

        if last:

            @pl.when(step == steps - 1)
            def _():
                for j in range(4):
                    base = (place_ref[0] ^ j) * part_rows
                    dest = far_ref if j & 1 else near_ref
                    for piece in range(pieces):
                        for crop in range(crops):
                            start = pl.multiple_of(
                                base + crop * images + (place_ref[2] ^ piece) * piece_images, piece_images
                            )
                            dest[j >> 1, piece, crop] = feat_ref[pl.ds(start, piece_images)]
                total = jnp.zeros((images, dim), F32)
                for group in range(groups):
                    base = group * part_rows
                    tbase = group * 2 * images
                    crop_rows = [
                        rows_ref[base + c * images : base + (c + 1) * images].astype(F32) for c in range(crops)
                    ]
                    shared = crop_rows[2]
                    for c in range(3, crops):
                        shared = shared + crop_rows[c]
                    total = total + targ_ref[tbase : tbase + images] * (crop_rows[1] + shared)
                    total = total + targ_ref[tbase + images : tbase + 2 * images] * (crop_rows[0] + shared)
                loss_ref[...] = jnp.sum(jnp.sum(total, axis=0, keepdims=True), axis=1, keepdims=True) + jnp.zeros(
                    (1, 128), F32
                )

    out_shape = [jax.ShapeDtypeStruct((dim // 2, columns // chunks), F32)] * 2
    out_specs = [pl.BlockSpec((dim // 2, width), lambda i, s: (0, i))] * 2
    operands = [protos, mass, column_sums, row_sum, rows, cols, offsets]
    in_specs = [
        pl.BlockSpec((dim, width), lambda i, s: (0, s[0] * total_steps + chunk * steps + i)),
    ] + [WHOLE] * 6
    aliases = {}
    scratch = []
    if not first:
        operands += list(carried)
        in_specs += [WHOLE] * 2
    if last:
        out_shape = out_shape + [jax.ShapeDtypeStruct((2, pieces, crops, piece_images, dim), F32)] * 2
        out_shape = out_shape + [jax.ShapeDtypeStruct((1, 128), F32)]
        out_specs = out_specs + [WHOLE] * 3
        if first:
            scratch += [pltpu.VMEM((row_count, dim), F32), pltpu.VMEM((teacher_rows, dim), F32)]
    else:
        out_shape = out_shape + [vmem((row_count, dim), F32), vmem((teacher_rows, dim), F32)]
        out_specs = out_specs + [WHOLE] * 2
        if not first:
            aliases = {8: 2, 9: 3}
    scratch += [
        pltpu.VMEM((row_count, width), BF16),
        pltpu.VMEM((teacher_rows, width), BF16),
        pltpu.VMEM((teacher_rows, 128), F32),
        pltpu.VMEM((dim, width), F32),
    ]
    return pl.pallas_call(
        kernel,
        grid_spec=pltpu.PrefetchScalarGridSpec(
            num_scalar_prefetch=1, grid=(steps,), in_specs=in_specs, out_specs=out_specs, scratch_shapes=scratch
        ),
        out_shape=out_shape,
        input_output_aliases=aliases,
        compiler_params=params(28),
        name="gradients",
    )(place, *operands)


def assemble(place, pieces):
    rows, width = pieces[0][0].shape
    chunks = len(pieces)
    columns = 4 * chunks * width

    def kernel(place_ref, *refs):
        out_ref = refs[-1]
        for chunk in range(chunks):
            for j in range(4):
                at = pl.multiple_of((place_ref[0] ^ j) * (chunks * width) + chunk * width, width)
                out_ref[:, pl.ds(at, width)] = refs[4 * chunk + j][...]

    return pl.pallas_call(
        kernel,
        in_specs=[SCALARS] + [WHOLE] * (4 * chunks),
        out_specs=WHOLE,
        out_shape=jax.ShapeDtypeStruct((rows, columns), F32),
        compiler_params=params(24),
        name="assemble",
    )(place, *[piece for chunk in pieces for piece in chunk])


def on_device(student_features, teacher_features, student_prototypes, teacher_prototypes):
    crops, images, dim = student_features.shape
    proto_local = student_prototypes.shape[1]
    batch_devices = lax.axis_size("batch")
    proto_devices = lax.axis_size("proto")
    batch_bits = bits_of(batch_devices)
    proto_bits = bits_of(proto_devices)
    images_all = images * batch_devices
    sample_number = teacher_features.shape[0] * images_all
    factor = 1.0 / (images_all * PAIRS * STUDENT_TEMP)
    batch_index = lax.axis_index("batch")
    proto_index = lax.axis_index("proto")
    core, top = 0, batch_bits - 1
    middle = list(range(1, top))
    place = ((batch_index >> top) & 1) * 2 + (batch_index & 1)
    own_images = images // proto_devices
    columns = proto_local // 4
    width = min(512, columns // CHUNKS)
    places = jnp.stack([place, batch_index, proto_index]).astype(jnp.int32)
    row_places = jnp.stack([place, proto_index]).astype(jnp.int32)

    unit_student, student_scale = unit_rows(student_features)
    unit_teacher, _ = unit_rows(teacher_features)
    teacher_own = unit_teacher.reshape(-1, dim)
    teacher_core = swap(teacher_own, "batch", core)
    teacher_far = swap(teacher_own, "batch", top)
    teacher_far_core = swap(teacher_far, "batch", core)

    own_rows = unit_student.reshape(crops * images, dim)
    sums = row_sums(own_rows, student_prototypes, 512)

    mass, column_sum = teacher_mass(
        places,
        [teacher_own, teacher_core, teacher_far, teacher_far_core],
        teacher_prototypes,
        columns,
        min(512, columns),
    )

    own_start = proto_index * own_images
    unit_own = lax.dynamic_slice_in_dim(unit_student, own_start, own_images, 1)
    scale_own = lax.dynamic_slice_in_dim(student_scale, own_start, own_images, 1)
    far = swap(unit_own, "batch", top)[None]
    for bit in range(proto_bits):
        far = jnp.concatenate([far, swap(far, "proto", bit)], axis=0)
    core_rows = swap(own_rows, "batch", core)
    far_core = swap(far, "batch", core)
    rows, cols = gather_rows(row_places, own_rows, core_rows, far, far_core, crops, images)

    all_sums = lax.dynamic_update_slice_in_dim(
        jnp.zeros((1, 4 * crops * images), F32), sums, place * (crops * images), 1
    )
    for bit in range(proto_bits):
        all_sums = all_sums + swap(all_sums, "proto", bit)
    all_sums = all_sums + swap(all_sums, "batch", top)
    all_sums = all_sums + swap(all_sums, "batch", core)
    offsets = row_offsets(all_sums, crops, images, factor)

    row_parts = None
    for sweep_index in range(SK_ITERS):
        if sweep_index:
            column_sum = column_pass(row_parts, mass, sample_number)
        for bit in middle[:-1]:
            column_sum = column_sum + swap(column_sum, "batch", bit)
        column_parts = (column_sum, swap(column_sum, "batch", middle[-1]))
        row_sum = row_pass(column_parts, mass)
        for bit in range(proto_bits):
            row_sum = row_sum + swap(row_sum, "proto", bit)
        row_sum = row_sum + swap(row_sum, "batch", top)
        row_parts = (row_sum, swap(row_sum, "batch", core))

    row_total = row_parts[0] + row_parts[1]
    column_total = column_parts[0] + column_parts[1]
    order = [0]
    for bit in [core, top] + middle[::-1]:
        order = order + [j | (1 << bit) for j in order]
    geometry = (crops, images, proto_devices, batch_devices, factor, order)
    carried = None
    pieces = []
    for chunk in range(CHUNKS):
        outs = gradients(
            places, chunk, CHUNKS, student_prototypes, mass, column_total, row_total, rows, cols, offsets,
            carried, geometry, width,
        )
        send, keep = outs[:2]
        carried = outs[2:]
        for bit in middle[:-1]:
            keep = keep + swap(send, "batch", bit)
            send = keep[keep.shape[0] // 2 :]
            keep = keep[: keep.shape[0] // 2]
        keep = keep + swap(send, "batch", middle[-1])
        half = keep.shape[0] // 2
        far_half = swap(keep[half:], "batch", top)
        near_half = keep[:half]
        quarter = half // 2
        from_core = swap(jnp.stack([near_half[quarter:], far_half[quarter:]]), "batch", core)
        pieces.append([near_half[:quarter], from_core[0], far_half[:quarter], from_core[1]])
    grad_prototypes = assemble(places, pieces)

    send, keep, loss_part = carried
    keep = keep + swap(send, "batch", core)
    totals = []
    for wing in range(2):
        part = keep[wing].reshape((2,) * proto_bits + (crops, own_images, dim))
        axes = list(range(proto_bits))
        axes = axes[wing % proto_bits :] + axes[: wing % proto_bits]
        for axis in axes:
            bit = proto_bits - 1 - axis
            near = lax.slice_in_dim(part, 0, 1, axis=axis)
            away = lax.slice_in_dim(part, 1, 2, axis=axis)
            part = near + swap(away, "proto", bit)
        totals.append(part.reshape(crops, own_images, dim))
    cot_own = totals[0] + swap(totals[1], "batch", top)
    grad_features = scale_own * (
        cot_own - unit_own * jnp.sum(unit_own * cot_own, axis=-1, keepdims=True)
    )

    own_sums = lax.dynamic_slice_in_dim(all_sums, place * (crops * images), crops * images, 1)
    pair_count = jnp.where(jnp.arange(crops * images) < 2 * images, F32(1.0), F32(2.0))
    norm_part = jnp.sum(pair_count * jnp.log(own_sums[0])) / proto_devices
    loss = norm_part - loss_part[:, :1] * (1.0 / (factor * STUDENT_TEMP))
    for bit in range(proto_bits):
        loss = loss + swap(loss, "proto", bit)
    for bit in range(batch_bits):
        loss = loss + swap(loss, "batch", bit)
    mean_loss = loss[0, 0] / (images_all * PAIRS)
    return (mean_loss, grad_features, grad_prototypes)


def solution(mesh):
    placed = (P(None, "batch", None), P(None, "batch", None), P(None, "proto"), P(None, "proto"))
    return jax.shard_map(
        on_device,
        mesh=mesh,
        in_specs=placed,
        out_specs=(P(), P(None, ("batch", "proto"), None), P("batch", "proto")),
        check_vma=False,
    )
```

```python
import math

import jax
import jax.numpy as jnp
from jax import lax
from jax.experimental import pallas as pl
from jax.experimental.pallas import tpu as pltpu
from jax.sharding import PartitionSpec as P


CLUSTER_NUMBER = 65536
SK_ITERS = 3
PAIRS = 18

STUDENT_TEMP = 0.1
TEACHER_TEMP = 0.07
NORM_EPS = 1e-06
LOG2E = math.log2(math.e)

CHUNKS = (1, 2, 2, 2, 1)
LOSS_ROWS = 8
MIB = 1 << 20
F32 = jnp.float32
BF16 = jnp.bfloat16
WHOLE = pl.BlockSpec(memory_space=pltpu.VMEM)
SCALARS = pl.BlockSpec(memory_space=pltpu.SMEM)


def vmem(shape, dtype):
    return pltpu.VMEM(shape, dtype)


def hbm(shape, dtype):
    return pltpu.HBM(shape, dtype)


def params():
    return pltpu.CompilerParams(vmem_limit_bytes=16 * MIB)


def cost(micros):
    return pl.CostEstimate(flops=int(micros * 1e9), transcendentals=0, bytes_accessed=int(micros * 1e6))


def exchange(value, axis, mask):
    size = lax.axis_size(axis)
    return lax.ppermute(value, axis, [(i, i ^ mask) for i in range(size)])


def swap(value, axis, bit):
    return exchange(value, axis, 1 << bit)


def bits_sum(value, axis, bits):
    for first in range(0, len(bits), 2):
        masks = [0]
        for bit in bits[first : first + 2]:
            masks += [mask | (1 << bit) for mask in masks]
        received = []
        for mask in masks[1:]:
            received.append(exchange(value, axis, mask))
        for part in received:
            value = value + part
    return value


def bits_of(size):
    return size.bit_length() - 1


def unit_rows(values):
    floats = values.astype(F32)
    inverse = lax.rsqrt(jnp.sum(floats * floats, axis=-1, keepdims=True) + NORM_EPS)
    return (floats * inverse, inverse)


def column_scale(floats):
    return lax.rsqrt(jnp.sum(floats * floats, axis=0, keepdims=True) + NORM_EPS)


def rows_to_lanes(partial):
    return jnp.concatenate(
        [
            jnp.sum(partial[i : i + 128].T, axis=0, keepdims=True)
            for i in range(0, partial.shape[0], 128)
        ],
        axis=1,
    )


def lanes_to_rows(values, start):
    return jnp.broadcast_to(values[:, start : start + 128], (128, 128)).T


def row_sums(place, unit, protos, width):
    rows, dim = unit.shape
    columns = protos.shape[1]
    steps = columns // width

    def kernel(place_ref, unit_ref, proto_ref, out_ref, rows_ref, sum_ref):
        step = pl.program_id(0)

        @pl.when(step == 0)
        def _():
            rows_ref[...] = unit_ref[...].astype(BF16)
            sum_ref[...] = jnp.zeros_like(sum_ref)

        for start in range(0, width, 512):
            floats = proto_ref[:, start : start + 512].astype(F32)
            proto_bf = (floats * column_scale(floats)).astype(BF16)
            cos = jnp.dot(rows_ref[...], proto_bf, preferred_element_type=F32)
            mass = jnp.exp2(cos * (LOG2E / STUDENT_TEMP))
            total = mass[:, :128]
            for lane in range(128, 512, 128):
                total = total + mass[:, lane : lane + 128]
            sum_ref[...] += total

        @pl.when(step == steps - 1)
        def _():
            out_ref[...] = jnp.zeros_like(out_ref)
            start = pl.multiple_of(place_ref[0] * rows, rows)
            out_ref[:, pl.ds(start, rows)] = rows_to_lanes(sum_ref[...])

    return pl.pallas_call(
        kernel,
        grid=(steps,),
        in_specs=[
            SCALARS,
            pl.BlockSpec((rows, dim), lambda i: (0, 0)),
            pl.BlockSpec((dim, width), lambda i: (0, i)),
        ],
        out_specs=pl.BlockSpec((1, 4 * rows), lambda i: (0, 0)),
        out_shape=jax.ShapeDtypeStruct((1, 4 * rows), F32),
        scratch_shapes=[pltpu.VMEM((rows, dim), BF16), pltpu.VMEM((rows, 128), F32)],
        compiler_params=params(),
        cost_estimate=cost(15),
        name="row_sums",
    )(place, unit, protos)


def teacher_mass(place, gathered, protos, columns, width):
    part_rows, dim = gathered[0].shape
    rows = part_rows * len(gathered)
    steps = columns // width

    def kernel(place_ref, *refs):
        parts = refs[: len(gathered)]
        proto_ref, mass_ref, sum_ref, rows_ref = refs[len(gathered) :]
        step = pl.program_id(0)

        @pl.when(step == 0)
        def _():
            for j, part in enumerate(parts):
                start = pl.multiple_of((place_ref[0] ^ j) * part_rows, part_rows)
                rows_ref[pl.ds(start, part_rows)] = part[...].astype(BF16)

        floats = proto_ref[...].astype(F32)
        proto_bf = (floats * column_scale(floats)).astype(BF16)
        at = pl.multiple_of(step * width, width)
        cos = jnp.dot(rows_ref[...], proto_bf, preferred_element_type=F32)
        mass = jnp.exp2(cos * (LOG2E / TEACHER_TEMP))
        mass_ref[:, pl.ds(at, width)] = mass
        sum_ref[...] = jnp.sum(mass, axis=0, keepdims=True)

    return pl.pallas_call(
        kernel,
        grid_spec=pltpu.PrefetchScalarGridSpec(
            num_scalar_prefetch=1,
            grid=(steps,),
            in_specs=[pl.BlockSpec((part_rows, dim), lambda i, s: (0, 0)) for _ in gathered]
            + [pl.BlockSpec((dim, width), lambda i, s: (0, s[0] * steps + i))],
            out_specs=[WHOLE, pl.BlockSpec((1, width), lambda i, s: (0, i))],
            scratch_shapes=[pltpu.VMEM((rows, dim), BF16)],
        ),
        out_shape=[vmem((rows, columns), F32), jax.ShapeDtypeStruct((1, columns), F32)],
        compiler_params=params(),
        cost_estimate=cost(5),
        name="teacher_mass",
    )(place, *gathered, protos)


def row_pass(column_parts, mass, extra):
    rows, columns = mass.shape
    extras = [] if extra is None else [extra]
    total_rows = rows + sum(part.shape[1] for part in extras)

    def kernel(a_ref, b_ref, mass_ref, *refs):
        out_ref = refs[-1]
        scale = 1.0 / (CLUSTER_NUMBER * (a_ref[...] + b_ref[...]))

        def block(index, carry):
            start = pl.multiple_of(index * 128, 128)
            total = jnp.zeros((128, 128), F32)
            for lane in range(0, columns, 128):
                total = total + (
                    mass_ref[pl.ds(start, 128), lane : lane + 128] * scale[:, lane : lane + 128]
                )
            out_ref[:, pl.ds(start, 128)] = jnp.sum(total.T, axis=0, keepdims=True)
            return carry

        lax.fori_loop(0, rows // 128, block, 0, unroll=2)
        if extras:
            out_ref[:, rows:] = refs[0][...]

    return pl.pallas_call(
        kernel,
        in_specs=[WHOLE] * (3 + len(extras)),
        out_specs=WHOLE,
        out_shape=jax.ShapeDtypeStruct((1, total_rows), F32),
        compiler_params=params(),
        cost_estimate=cost(1.5),
        name="row_pass",
    )(*column_parts, mass, *extras)


def column_pass(row_parts, mass, sample_number):
    rows, columns = mass.shape

    def kernel(a_ref, b_ref, mass_ref, out_ref, scale_ref):
        scale = 1.0 / (sample_number * (a_ref[:, :rows] + b_ref[:, :rows]))
        for start in range(0, rows, 128):
            scale_ref[start : start + 128] = lanes_to_rows(scale, start)

        def block(index, carry):
            lane = pl.multiple_of(index * 256, 256)
            total = jnp.zeros((8, 256), F32)
            for start in range(0, rows, 128):
                scales = jnp.concatenate([scale_ref[start : start + 128]] * 2, axis=1)
                term = mass_ref[start : start + 128, pl.ds(lane, 256)] * scales
                total = total + jnp.sum(term.reshape(16, 8, 256), axis=0)
            out_ref[:, pl.ds(lane, 256)] = jnp.sum(total, axis=0, keepdims=True)
            return carry

        lax.fori_loop(0, columns // 256, block, 0, unroll=2)

    return pl.pallas_call(
        kernel,
        in_specs=[WHOLE] * 3,
        out_specs=WHOLE,
        out_shape=jax.ShapeDtypeStruct((1, columns), F32),
        scratch_shapes=[pltpu.VMEM((rows, 128), F32)],
        compiler_params=params(),
        cost_estimate=cost(1.5),
        name="column_pass",
    )(*row_parts, mass)


def gather_rows(place, own, core, far, far_core, crops, images):
    dim = own.shape[1]
    part_rows = crops * images
    pieces, _, piece_images, _ = far.shape
    rows = 4 * part_rows

    def kernel(place_ref, own_ref, core_ref, far_ref, far_core_ref, rows_ref, cols_ref, work_ref):
        def store(j, values):
            start = pl.multiple_of((place_ref[0] ^ j) * part_rows, part_rows)
            rows_ref[pl.ds(start, part_rows)] = values.astype(BF16)
            cols_ref[:, pl.ds(start, part_rows)] = values.T.astype(BF16)

        store(0, own_ref[...])
        store(1, core_ref[...])
        for j, ref in ((2, far_ref), (3, far_core_ref)):
            for piece in range(pieces):
                offset = (place_ref[1] ^ piece) * piece_images
                for crop in range(crops):
                    at = pl.multiple_of(crop * images + offset, piece_images)
                    work_ref[pl.ds(at, piece_images)] = ref[piece, crop]
            store(j, work_ref[...])

    return pl.pallas_call(
        kernel,
        in_specs=[SCALARS] + [WHOLE] * 4,
        out_specs=[WHOLE] * 2,
        out_shape=[vmem((rows, dim), BF16), vmem((dim, rows), BF16)],
        scratch_shapes=[pltpu.VMEM((part_rows, dim), F32)],
        compiler_params=params(),
        cost_estimate=cost(3),
        name="gather_rows",
    )(place, own, core, far, far_core)


def row_offsets(parts, skip, crops, images, factor):
    rows = parts[0].shape[1] - skip

    def kernel(a_ref, b_ref, out_ref, norm_ref, sums_ref):
        sums_ref[...] = a_ref[:, skip:] + b_ref[:, skip:]

        def block(index, total):
            start = pl.multiple_of(index * 128, 128)
            pair_count = jnp.where((start // images) % crops < 2, F32(1.0), F32(2.0))
            sums = sums_ref[:, pl.ds(start, 128)]
            out_ref[pl.ds(start, 128)] = lanes_to_rows(jnp.log2((pair_count * factor) / sums), 0)
            return total + pair_count * jnp.log(sums)

        total = lax.fori_loop(0, rows // 128, block, jnp.zeros((1, 128), F32))
        norm_ref[...] = jnp.sum(total, axis=1, keepdims=True) + jnp.zeros((1, 128), F32)

    return pl.pallas_call(
        kernel,
        in_specs=[WHOLE] * 2,
        out_specs=[WHOLE] * 2,
        out_shape=[vmem((rows, 128), F32), jax.ShapeDtypeStruct((1, 128), F32)],
        scratch_shapes=[pltpu.VMEM((1, rows), F32)],
        compiler_params=params(),
        cost_estimate=cost(1),
        name="row_offsets",
    )(*parts)


def gradients(place, steps, first, last, protos, mass, column_sums, row_sum, rows, cols, offsets, norm_sum, carried, geometry):
    crops, images, pieces, blocks, factor, order = geometry
    dim = protos.shape[0]
    half = dim // 2
    out_rows = half + (LOSS_ROWS if last else 0)
    row_count = rows.shape[0]
    teacher_rows, columns = mass.shape
    groups = teacher_rows // (2 * images)
    part_rows = crops * images
    piece_images = images // pieces
    total_steps = sum(CHUNKS)
    width = columns // total_steps
    block_rows = dim // blocks

    def kernel(place_ref, *refs):
        refs = list(refs)
        proto_ref, mass_ref, csum_ref, rsum_ref, rows_ref, cols_ref, offs_ref = refs[:7]
        refs = refs[7:]
        if last:
            norm_ref = refs.pop(0)
        if not first:
            feat_in, targ_in = refs[:2]
            refs = refs[2:]
        send_ref, keep_ref = refs[:2]
        refs = refs[2:]
        if last:
            far_ref, near_ref = refs[:2]
            refs = refs[2:]
            sem_ref = refs.pop()
            feat_ref, targ_ref = feat_in, targ_in
        else:
            feat_ref, targ_ref = refs[:2]
            refs = refs[2:]
        grad_ref, tbf_ref, rscale_ref, weight_ref, *cos_refs = refs
        step = pl.program_id(0)

        @pl.when(step == 0)
        def _():
            scale = factor / rsum_ref[...]
            for start in range(0, teacher_rows, 128):
                rscale_ref[start : start + 128] = lanes_to_rows(scale, start)
            if first:
                feat_ref[...] = jnp.zeros_like(feat_ref)
                targ_ref[...] = jnp.zeros_like(targ_ref)

        at = pl.multiple_of((place_ref[3] + step) * width, width)
        floats = proto_ref[...].astype(F32)
        inverse = column_scale(floats)
        unit = floats * inverse
        proto_bf = unit.astype(BF16)
        proto_t = unit.T.astype(BF16)
        cscale = 1.0 / (CLUSTER_NUMBER * csum_ref[:, pl.ds(at, width)])

        for group in range(groups):
            base = group * part_rows
            tbase = group * 2 * images
            cos_ref = cos_refs[group % 2]
            cos_ref[...] = jnp.dot(rows_ref[base : base + part_rows], proto_bf, preferred_element_type=F32)
            for lane in range(0, width, 128):
                lanes = slice(lane, lane + 128)
                for image in range(0, images, 64):
                    pair = []
                    for wide in range(2):
                        start = tbase + wide * images + image
                        target = (
                            mass_ref[start : start + 64, pl.ds(at + lane, 128)]
                            * rscale_ref[start : start + 64]
                            * cscale[:, lanes]
                        )
                        tbf_ref[start : start + 64, lanes] = target.astype(BF16)
                        pair.append(target)
                    both = pair[0] + pair[1]
                    for crop in range(crops):
                        start = crop * images + image
                        power = cos_ref[start : start + 64, lanes] * (LOG2E / STUDENT_TEMP)
                        prob = jnp.exp2(power + offs_ref[base + start : base + start + 64])
                        target = pair[1] if crop == 0 else pair[0] if crop == 1 else both
                        grad_ref[base + start : base + start + 64, lanes] = (prob - target).astype(BF16)
            product = jnp.dot(grad_ref[base : base + part_rows], proto_t, preferred_element_type=F32)
            feat_ref[group] += product.reshape(crops, images, dim)
        copies = []
        if last:
            for j in range(4):
                dest = far_ref if j & 1 else near_ref
                for piece in range(pieces):
                    start = pl.multiple_of((place_ref[2] ^ piece) * piece_images, piece_images)
                    copies.append(
                        pltpu.make_async_copy(
                            feat_ref.at[place_ref[0] ^ j, :, pl.ds(start, piece_images)],
                            dest.at[j >> 1, piece],
                            sem_ref.at[len(copies)],
                        )
                    )
                    copies[-1].start()
        targ_ref[...] += jnp.dot(tbf_ref[...], proto_t, preferred_element_type=F32)
        weight = jnp.dot(cols_ref[...], grad_ref[...], preferred_element_type=F32)
        curvature = jnp.sum(proto_bf.astype(F32) * weight, axis=0, keepdims=True)
        weight_ref[...] = inverse * (weight - unit * curvature)
        for position, j in enumerate(order):
            start = pl.multiple_of((place_ref[1] ^ j) * block_rows, block_rows)
            dest, index = (keep_ref, position) if position < blocks // 2 else (send_ref, position - blocks // 2)
            dest[index * block_rows : (index + 1) * block_rows] = weight_ref[pl.ds(start, block_rows)]

        if last:
            total = jnp.zeros((images, dim), F32)
            for group in range(groups):
                base = group * part_rows
                tbase = group * 2 * images
                crop_rows = [
                    rows_ref[base + c * images : base + (c + 1) * images].astype(F32) for c in range(crops)
                ]
                shared = crop_rows[2]
                for c in range(3, crops):
                    shared = shared + crop_rows[c]
                total = total + targ_ref[tbase : tbase + images] * (crop_rows[1] + shared)
                total = total + targ_ref[tbase + images : tbase + 2 * images] * (crop_rows[0] + shared)
            product = jnp.sum(jnp.sum(total, axis=0, keepdims=True), axis=1, keepdims=True)
            loss = norm_ref[:, :1] * (1.0 / (4 * pieces)) - product * (1.0 / (factor * STUDENT_TEMP))
            keep_ref[half:] = loss + jnp.zeros((LOSS_ROWS, width), F32)
            send_ref[half:] = loss + jnp.zeros((LOSS_ROWS, width), F32)
            for copy in copies:
                copy.wait()

    out_shape = [hbm((out_rows, steps * width), F32)] * 2
    out_specs = [pl.BlockSpec((out_rows, width), lambda i, s: (0, i))] * 2
    operands = [protos, mass, column_sums, row_sum, rows, cols, offsets]
    in_specs = [
        pl.BlockSpec((dim, width), lambda i, s: (0, s[0] * total_steps + s[3] + i)),
    ] + [WHOLE] * 6
    aliases = {}
    scratch = []
    if last:
        operands.append(norm_sum)
        in_specs.append(WHOLE)
    if not first:
        operands += list(carried)
        in_specs += [WHOLE] * 2
    if last:
        shape = (2, pieces, crops, piece_images, dim)
        out_shape = out_shape + [hbm(shape, F32)] * 2
        out_specs = out_specs + [pl.BlockSpec(memory_space=pl.ANY)] * 2
    else:
        out_shape = out_shape + [vmem((groups, crops, images, dim), F32), vmem((teacher_rows, dim), F32)]
        out_specs = out_specs + [WHOLE] * 2
        if not first:
            aliases = {8: 2, 9: 3}
    scratch += [
        pltpu.VMEM((row_count, width), BF16),
        pltpu.VMEM((teacher_rows, width), BF16),
        pltpu.VMEM((teacher_rows, 128), F32),
        pltpu.VMEM((dim, width), F32),
        pltpu.VMEM((part_rows, width), F32),
        pltpu.VMEM((part_rows, width), F32),
    ]
    if last:
        assert steps == 1 and not first
        scratch.append(pltpu.SemaphoreType.DMA((4 * pieces,)))
    return pl.pallas_call(
        kernel,
        grid_spec=pltpu.PrefetchScalarGridSpec(
            num_scalar_prefetch=1, grid=(steps,), in_specs=in_specs, out_specs=out_specs, scratch_shapes=scratch
        ),
        out_shape=out_shape,
        input_output_aliases=aliases,
        compiler_params=params(),
        cost_estimate=cost(10),
        name="gradients",
    )(place, *operands)


def assemble(place, pieces):
    rows = pieces[0][0].shape[0]
    widths = [piece[0].shape[1] for piece in pieces]
    chunks = len(pieces)
    quarter = sum(widths)
    columns = 4 * quarter

    def kernel(place_ref, *refs):
        out_ref = refs[-1]
        offset = 0
        for chunk, width in enumerate(widths):
            for j in range(4):
                at = pl.multiple_of((place_ref[0] ^ j) * quarter + offset, 128)
                out_ref[:, pl.ds(at, width)] = refs[4 * chunk + j][...]
            offset += width

    return pl.pallas_call(
        kernel,
        in_specs=[SCALARS] + [WHOLE] * (4 * chunks),
        out_specs=WHOLE,
        out_shape=jax.ShapeDtypeStruct((rows, columns), F32),
        compiler_params=params(),
        name="assemble",
    )(place, *[piece for chunk in pieces for piece in chunk])


def step_on_device(student_features, teacher_features, student_prototypes, teacher_prototypes):
    student_prototypes = pltpu.with_memory_space_constraint(student_prototypes, pltpu.HBM)
    teacher_prototypes = pltpu.with_memory_space_constraint(teacher_prototypes, pltpu.HBM)
    crops, images, dim = student_features.shape
    proto_local = student_prototypes.shape[1]
    batch_devices = lax.axis_size("batch")
    proto_devices = lax.axis_size("proto")
    batch_bits = bits_of(batch_devices)
    proto_bits = bits_of(proto_devices)
    images_all = images * batch_devices
    sample_number = teacher_features.shape[0] * images_all
    factor = 1.0 / (images_all * PAIRS * STUDENT_TEMP)
    batch_index = lax.axis_index("batch")
    proto_index = lax.axis_index("proto")
    core, top = 0, batch_bits - 1
    middle = list(range(1, top))
    place = ((batch_index >> top) & 1) * 2 + (batch_index & 1)
    own_images = images // proto_devices
    columns = proto_local // 4
    places = jnp.stack([place, batch_index, proto_index]).astype(jnp.int32)
    chunk_places = [
        jnp.stack([place, batch_index, proto_index, jnp.int32(sum(CHUNKS[:chunk]))]).astype(jnp.int32)
        for chunk in range(len(CHUNKS))
    ]
    row_places = jnp.stack([place, proto_index]).astype(jnp.int32)

    unit_student, student_scale = unit_rows(student_features)
    unit_teacher, _ = unit_rows(teacher_features)
    teacher_own = unit_teacher.reshape(-1, dim)
    teacher_core = swap(teacher_own, "batch", core)
    teacher_far = swap(teacher_own, "batch", top)
    teacher_far_core = swap(teacher_far, "batch", core)

    own_rows = unit_student.reshape(crops * images, dim)
    all_sums = row_sums(places, own_rows, student_prototypes, min(2048, proto_local))

    mass, column_sum = teacher_mass(
        places,
        [teacher_own, teacher_core, teacher_far, teacher_far_core],
        teacher_prototypes,
        columns,
        min(512, columns),
    )

    own_start = proto_index * own_images
    unit_own = lax.dynamic_slice_in_dim(unit_student, own_start, own_images, 1)
    scale_own = lax.dynamic_slice_in_dim(student_scale, own_start, own_images, 1)
    far = swap(unit_own, "batch", top)[None]
    for bit in range(proto_bits):
        received = swap(far, "proto", bit)
        far = jnp.concatenate([far, received], axis=0)
    core_rows = swap(own_rows, "batch", core)
    far_core = swap(far, "batch", core)
    rows, cols = gather_rows(row_places, own_rows, core_rows, far, far_core, crops, images)

    row_parts = None
    for sweep_index in range(SK_ITERS):
        if sweep_index:
            column_sum = column_pass(row_parts, mass, sample_number)
        for bit in middle[:-1]:
            column_sum = column_sum + swap(column_sum, "batch", bit)
        column_parts = (column_sum, swap(column_sum, "batch", middle[-1]))
        row_sum = row_pass(column_parts, mass, None if sweep_index else all_sums)
        row_sum = bits_sum(row_sum, "proto", range(proto_bits))
        received = swap(row_sum, "batch", top)
        row_sum = row_sum + received
        row_parts = (row_sum, swap(row_sum, "batch", core))
        if sweep_index == 0:
            offsets, norm_sum = row_offsets(row_parts, mass.shape[0], crops, images, factor)

    row_total = row_parts[0] + row_parts[1]
    column_total = column_parts[0] + column_parts[1]
    order = [0]
    for bit in [core, top] + middle[::-1]:
        order = order + [j | (1 << bit) for j in order]
    geometry = (crops, images, proto_devices, batch_devices, factor, order)
    carried = None
    pieces = []
    for chunk, steps in enumerate(CHUNKS):
        outs = gradients(
            chunk_places[chunk], steps, chunk == 0, chunk == len(CHUNKS) - 1, student_prototypes, mass,
            column_total, row_total, rows, cols, offsets, norm_sum, carried, geometry,
        )
        send, keep = outs[:2]
        carried = outs[2:]
        loss_rows = LOSS_ROWS if chunk == len(CHUNKS) - 1 else 0
        for bit in middle[:-1]:
            keep = keep + swap(send, "batch", bit)
            end = keep.shape[0] - loss_rows
            send = keep[end // 2 :]
            keep = jnp.concatenate([keep[: end // 2], keep[end:]], axis=0)
        half = (keep.shape[0] - loss_rows) // 2
        quarter = half // 2
        received = swap(send, "batch", middle[-1])
        far_send = keep[half:] + received[half:]
        near_own = keep[:quarter] + received[:quarter]
        near_core = keep[quarter:half] + received[quarter:half]
        far_half = swap(far_send, "batch", top)
        near_core = swap(near_core, "batch", core)
        far_core = far_half[quarter:half]
        if loss_rows:
            loss = far_send[half:] + far_half[half:]
            far_core = jnp.concatenate([far_core, loss], axis=0)
        far_core = swap(far_core, "batch", core)
        if loss_rows:
            loss = (loss + far_core[quarter:])[:1, :128]
        pieces.append([near_own, near_core, far_half[:quarter], far_core[:quarter]])
    grad_prototypes = assemble(places, pieces)

    send, keep = carried
    received = swap(send, "batch", core)
    totals = []
    for wing in range(2):
        part = (keep[wing] + received[wing]).reshape((2,) * proto_bits + (crops, own_images, dim))
        axes = list(range(proto_bits))
        axes = axes[wing % proto_bits :] + axes[: wing % proto_bits]
        for axis in axes:
            bit = proto_bits - 1 - axis
            near = lax.slice_in_dim(part, 0, 1, axis=axis)
            away = lax.slice_in_dim(part, 1, 2, axis=axis)
            part = near + swap(away, "proto", bit)
        totals.append(part.reshape(crops, own_images, dim))
    cot_own = totals[0] + swap(totals[1], "batch", top)
    grad_features = scale_own * (
        cot_own - unit_own * jnp.sum(unit_own * cot_own, axis=-1, keepdims=True)
    )

    loss = bits_sum(loss, "proto", range(proto_bits))
    mean_loss = loss[0, 0] / (images_all * PAIRS)
    return (mean_loss, grad_features, grad_prototypes)


def solution(mesh):
    placed = (P(None, "batch", None), P(None, "batch", None), P(None, "proto"), P(None, "proto"))
    return jax.shard_map(
        step_on_device,
        mesh=mesh,
        in_specs=placed,
        out_specs=(P(), P(None, ("batch", "proto"), None), P("batch", "proto")),
        check_vma=False,
    )
```

```python
import math

import jax
import jax.numpy as jnp
from jax import lax
from jax.experimental import pallas as pl
from jax.experimental.pallas import tpu as pltpu
from jax.sharding import PartitionSpec as P


CLUSTER_NUMBER = 65536
SK_ITERS = 3
BATCH = "batch"
PROTO = "proto"
PAIRS = 18

STUDENT_TEMP = 0.1
TEACHER_TEMP = 0.07
NORM_EPS = 1e-06
LOG2E = math.log2(math.e)

CHUNKS = (1, 2, 2, 2, 1)
LOSS_ROWS = 8
MIB = 1 << 20
F32 = jnp.float32
BF16 = jnp.bfloat16
WHOLE = pl.BlockSpec(memory_space=pltpu.VMEM)
SCALARS = pl.BlockSpec(memory_space=pltpu.SMEM)


def vmem(shape, dtype):
    return pltpu.VMEM(shape, dtype)


def hbm(shape, dtype):
    return pltpu.HBM(shape, dtype)


def params():
    return pltpu.CompilerParams(vmem_limit_bytes=16 * MIB)


def cost(micros):
    return pl.CostEstimate(flops=int(micros * 1e9), transcendentals=0, bytes_accessed=int(micros * 1e6))


def exchange(value, axis, mask):
    size = lax.axis_size(axis)
    return lax.ppermute(value, axis, [(i, i ^ mask) for i in range(size)])


def swap(value, axis, bit):
    return exchange(value, axis, 1 << bit)


def bits_sum(value, axis, bits):
    for first in range(0, len(bits), 2):
        masks = [0]
        for bit in bits[first : first + 2]:
            masks += [mask | (1 << bit) for mask in masks]
        received = []
        for mask in masks[1:]:
            received.append(exchange(value, axis, mask))
        for part in received:
            value = value + part
    return value


def bits_of(size):
    return size.bit_length() - 1


def unit_values(values):
    def kernel(in_ref, out_ref):
        floats = in_ref[...].astype(F32)
        out_ref[...] = floats * lax.rsqrt(jnp.sum(floats * floats, axis=1, keepdims=True) + NORM_EPS)

    return pl.pallas_call(
        kernel,
        in_specs=[WHOLE],
        out_specs=WHOLE,
        out_shape=jax.ShapeDtypeStruct(values.shape, F32),
        compiler_params=params(),
        cost_estimate=cost(1),
        name="units",
    )(values)


def column_scale(floats):
    return lax.rsqrt(jnp.sum(floats * floats, axis=0, keepdims=True) + NORM_EPS)


def rows_to_lanes(partial):
    return jnp.concatenate(
        [
            jnp.sum(partial[i : i + 128].T, axis=0, keepdims=True)
            for i in range(0, partial.shape[0], 128)
        ],
        axis=1,
    )


def lanes_to_rows(values, start):
    return jnp.broadcast_to(values[:, start : start + 128], (128, 128)).T


def row_sums(place, unit, protos, width):
    rows, dim = unit.shape
    columns = protos.shape[1]
    steps = columns // width

    def kernel(place_ref, unit_ref, proto_ref, out_ref, rows_ref, sum_ref):
        step = pl.program_id(0)

        @pl.when(step == 0)
        def _():
            rows_ref[...] = unit_ref[...].astype(BF16)
            sum_ref[...] = jnp.zeros_like(sum_ref)

        for start in range(0, width, 512):
            floats = proto_ref[:, start : start + 512].astype(F32)
            proto_bf = (floats * column_scale(floats)).astype(BF16)
            cos = jnp.dot(rows_ref[...], proto_bf, preferred_element_type=F32)
            mass = jnp.exp2(cos * (LOG2E / STUDENT_TEMP))
            total = mass[:, :128]
            for lane in range(128, 512, 128):
                total = total + mass[:, lane : lane + 128]
            sum_ref[...] += total

        @pl.when(step == steps - 1)
        def _():
            out_ref[...] = jnp.zeros_like(out_ref)
            start = pl.multiple_of(place_ref[0] * rows, rows)
            out_ref[:, pl.ds(start, rows)] = rows_to_lanes(sum_ref[...])

    return pl.pallas_call(
        kernel,
        grid=(steps,),
        in_specs=[
            SCALARS,
            pl.BlockSpec((rows, dim), lambda i: (0, 0)),
            pl.BlockSpec((dim, width), lambda i: (0, i)),
        ],
        out_specs=pl.BlockSpec((1, 4 * rows), lambda i: (0, 0)),
        out_shape=jax.ShapeDtypeStruct((1, 4 * rows), F32),
        scratch_shapes=[pltpu.VMEM((rows, dim), BF16), pltpu.VMEM((rows, 128), F32)],
        compiler_params=params(),
        cost_estimate=cost(15),
        name="row_sums",
    )(place, unit, protos)


def teacher_mass(place, gathered, protos, columns, width):
    part_rows, dim = gathered[0].shape
    rows = part_rows * len(gathered)
    steps = columns // width

    def kernel(place_ref, *refs):
        parts = refs[: len(gathered)]
        proto_ref, mass_ref, sum_ref, rows_ref = refs[len(gathered) :]
        step = pl.program_id(0)

        @pl.when(step == 0)
        def _():
            for j, part in enumerate(parts):
                start = pl.multiple_of((place_ref[0] ^ j) * part_rows, part_rows)
                rows_ref[pl.ds(start, part_rows)] = part[...].astype(BF16)

        at = pl.multiple_of(step * width, width)
        part = min(512, width)
        for start in range(0, width, part):
            floats = proto_ref[:, start : start + part].astype(F32)
            proto_bf = (floats * column_scale(floats)).astype(BF16)
            cos = jnp.dot(rows_ref[...], proto_bf, preferred_element_type=F32)
            mass = jnp.exp2(cos * (LOG2E / TEACHER_TEMP))
            mass_ref[:, pl.ds(at + start, part)] = mass
            sum_ref[:, start : start + part] = jnp.sum(mass, axis=0, keepdims=True)

    return pl.pallas_call(
        kernel,
        grid_spec=pltpu.PrefetchScalarGridSpec(
            num_scalar_prefetch=1,
            grid=(steps,),
            in_specs=[pl.BlockSpec((part_rows, dim), lambda i, s: (0, 0)) for _ in gathered]
            + [pl.BlockSpec((dim, width), lambda i, s: (0, s[0] * steps + i))],
            out_specs=[WHOLE, pl.BlockSpec((1, width), lambda i, s: (0, i))],
            scratch_shapes=[pltpu.VMEM((rows, dim), BF16)],
        ),
        out_shape=[vmem((rows, columns), F32), jax.ShapeDtypeStruct((1, columns), F32)],
        compiler_params=params(),
        cost_estimate=cost(5),
        name="teacher_mass",
    )(place, *gathered, protos)


def row_pass(column_parts, mass, extra):
    rows, columns = mass.shape
    extras = [] if extra is None else [extra]
    total_rows = rows + sum(part.shape[1] for part in extras)

    def kernel(a_ref, b_ref, mass_ref, *refs):
        out_ref = refs[-1]
        scale = 1.0 / (CLUSTER_NUMBER * (a_ref[...] + b_ref[...]))

        def block(index, carry):
            start = pl.multiple_of(index * 128, 128)
            total = jnp.zeros((128, 128), F32)
            for lane in range(0, columns, 128):
                total = total + (
                    mass_ref[pl.ds(start, 128), lane : lane + 128] * scale[:, lane : lane + 128]
                )
            out_ref[:, pl.ds(start, 128)] = jnp.sum(total.T, axis=0, keepdims=True)
            return carry

        lax.fori_loop(0, rows // 128, block, 0, unroll=2)
        if extras:
            out_ref[:, rows:] = refs[0][...]

    return pl.pallas_call(
        kernel,
        in_specs=[WHOLE] * (3 + len(extras)),
        out_specs=WHOLE,
        out_shape=jax.ShapeDtypeStruct((1, total_rows), F32),
        compiler_params=params(),
        cost_estimate=cost(1.5),
        name="row_pass",
    )(*column_parts, mass, *extras)


def column_pass(row_parts, mass, sample_number):
    rows, columns = mass.shape

    def kernel(a_ref, b_ref, mass_ref, out_ref, scale_ref):
        scale = 1.0 / (sample_number * (a_ref[:, :rows] + b_ref[:, :rows]))
        for start in range(0, rows, 128):
            scale_ref[start : start + 128] = lanes_to_rows(scale, start)

        def block(index, carry):
            lane = pl.multiple_of(index * 256, 256)
            total = jnp.zeros((8, 256), F32)
            for start in range(0, rows, 128):
                scales = jnp.concatenate([scale_ref[start : start + 128]] * 2, axis=1)
                term = mass_ref[start : start + 128, pl.ds(lane, 256)] * scales
                total = total + jnp.sum(term.reshape(16, 8, 256), axis=0)
            out_ref[:, pl.ds(lane, 256)] = jnp.sum(total, axis=0, keepdims=True)
            return carry

        lax.fori_loop(0, columns // 256, block, 0, unroll=2)

    return pl.pallas_call(
        kernel,
        in_specs=[WHOLE] * 3,
        out_specs=WHOLE,
        out_shape=jax.ShapeDtypeStruct((1, columns), F32),
        scratch_shapes=[pltpu.VMEM((rows, 128), F32)],
        compiler_params=params(),
        cost_estimate=cost(1.5),
        name="column_pass",
    )(*row_parts, mass)


def gather_rows(place, own, core, far, far_core, crops, images):
    dim = own.shape[1]
    part_rows = crops * images
    pieces, _, piece_images, _ = far.shape
    rows = 4 * part_rows

    def kernel(place_ref, own_ref, core_ref, far_ref, far_core_ref, rows_ref, cols_ref, work_ref):
        def store(j, values):
            start = pl.multiple_of((place_ref[0] ^ j) * part_rows, part_rows)
            rows_ref[pl.ds(start, part_rows)] = values.astype(BF16)
            cols_ref[:, pl.ds(start, part_rows)] = values.T.astype(BF16)

        store(0, own_ref[...])
        store(1, core_ref[...])
        for j, ref in ((2, far_ref), (3, far_core_ref)):

            def move(crop, carry, ref=ref):
                for piece in range(pieces):
                    offset = (place_ref[1] ^ piece) * piece_images
                    at = pl.multiple_of(crop * images + offset, piece_images)
                    work_ref[pl.ds(at, piece_images)] = ref[piece, crop]
                return carry

            lax.fori_loop(0, crops, move, 0)
            store(j, work_ref[...])

    return pl.pallas_call(
        kernel,
        in_specs=[SCALARS] + [WHOLE] * 4,
        out_specs=[WHOLE] * 2,
        out_shape=[vmem((rows, dim), BF16), vmem((dim, rows), BF16)],
        scratch_shapes=[pltpu.VMEM((part_rows, dim), F32)],
        compiler_params=params(),
        cost_estimate=cost(3),
        name="gather_rows",
    )(place, own, core, far, far_core)


def row_offsets(parts, skip, crops, images, factor):
    rows = parts[0].shape[1] - skip

    def kernel(a_ref, b_ref, out_ref, norm_ref, sums_ref):
        sums_ref[...] = a_ref[:, skip:] + b_ref[:, skip:]

        def block(index, total):
            start = pl.multiple_of(index * 128, 128)
            pair_count = jnp.where((start // images) % crops < 2, F32(1.0), F32(2.0))
            sums = sums_ref[:, pl.ds(start, 128)]
            out_ref[pl.ds(start, 128)] = lanes_to_rows(jnp.log2((pair_count * factor) / sums), 0)
            return total + pair_count * jnp.log(sums)

        total = lax.fori_loop(0, rows // 128, block, jnp.zeros((1, 128), F32), unroll=10)
        norm_ref[...] = jnp.sum(total, axis=1, keepdims=True) + jnp.zeros((1, 128), F32)

    return pl.pallas_call(
        kernel,
        in_specs=[WHOLE] * 2,
        out_specs=[WHOLE] * 2,
        out_shape=[vmem((rows, 128), F32), jax.ShapeDtypeStruct((1, 128), F32)],
        scratch_shapes=[pltpu.VMEM((1, rows), F32)],
        compiler_params=params(),
        cost_estimate=cost(1),
        name="row_offsets",
    )(*parts)


def gradients(place, steps, first, last, protos, mass, column_sums, row_sum, rows, cols, offsets, norm_sum, carried, geometry):
    crops, images, pieces, blocks, factor, order = geometry
    dim = protos.shape[0]
    half = dim // 2
    out_rows = half + (LOSS_ROWS if last else 0)
    row_count = rows.shape[0]
    teacher_rows, columns = mass.shape
    groups = teacher_rows // (2 * images)
    part_rows = crops * images
    piece_images = images // pieces
    total_steps = sum(CHUNKS)
    width = columns // total_steps
    block_rows = dim // blocks

    def kernel(place_ref, *refs):
        refs = list(refs)
        proto_ref, mass_ref, csum_ref, rsum_ref, rows_ref, cols_ref, offs_ref = refs[:7]
        refs = refs[7:]
        if last:
            norm_ref = refs.pop(0)
        if not first:
            feat_in, targ_in = refs[:2]
            refs = refs[2:]
        send_ref, keep_ref = refs[:2]
        refs = refs[2:]
        if last:
            wing_refs = refs[:4]
            refs = refs[4:]
            sem_ref = refs.pop()
            feat_ref, targ_ref = feat_in, targ_in
        else:
            feat_ref, targ_ref = refs[:2]
            refs = refs[2:]
        grad_ref, tbf_ref, rscale_ref, weight_ref, *cos_refs = refs
        step = pl.program_id(0)

        @pl.when(step == 0)
        def _():
            scale = factor / rsum_ref[...]
            for start in range(0, teacher_rows, 128):
                rscale_ref[start : start + 128] = lanes_to_rows(scale, start)
            if first:

                def clear(crop, carry):
                    feat_ref[:, pl.ds(crop, 1)] = jnp.zeros((groups, 1, images, dim), F32)
                    return carry

                lax.fori_loop(0, crops, clear, 0)
                targ_ref[...] = jnp.zeros_like(targ_ref)

        at = pl.multiple_of((place_ref[3] + step) * width, width)
        floats = proto_ref[...].astype(F32)
        inverse = column_scale(floats)
        unit = floats * inverse
        proto_bf = unit.astype(BF16)
        proto_t = unit.T.astype(BF16)
        cscale = 1.0 / (CLUSTER_NUMBER * csum_ref[:, pl.ds(at, width)])

        for group in range(groups):
            base = group * part_rows
            tbase = group * 2 * images
            cos_ref = cos_refs[group % 2]
            cos_ref[...] = jnp.dot(rows_ref[base : base + part_rows], proto_bf, preferred_element_type=F32)
            for lane in range(0, width, 128):
                lanes = slice(lane, lane + 128)
                for image in range(0, images, 64):
                    pair = []
                    for wide in range(2):
                        start = tbase + wide * images + image
                        target = (
                            mass_ref[start : start + 64, pl.ds(at + lane, 128)]
                            * rscale_ref[start : start + 64]
                            * cscale[:, lanes]
                        )
                        tbf_ref[start : start + 64, lanes] = target.astype(BF16)
                        pair.append(target)
                    both = pair[0] + pair[1]
                    for crop in range(crops):
                        start = crop * images + image
                        power = cos_ref[start : start + 64, lanes] * (LOG2E / STUDENT_TEMP)
                        prob = jnp.exp2(power + offs_ref[base + start : base + start + 64])
                        target = pair[1] if crop == 0 else pair[0] if crop == 1 else both
                        grad_ref[base + start : base + start + 64, lanes] = (prob - target).astype(BF16)
            product = jnp.dot(grad_ref[base : base + part_rows], proto_t, preferred_element_type=F32)
            feat_ref[group] += product.reshape(crops, images, dim)
        copies = []
        if last:
            for j in range(4):
                dest = wing_refs[(j >> 1) + (0 if j & 1 else 2)]
                for piece in range(pieces):
                    start = pl.multiple_of((place_ref[2] ^ piece) * piece_images, piece_images)
                    copies.append(
                        pltpu.make_async_copy(
                            feat_ref.at[place_ref[0] ^ j, :, pl.ds(start, piece_images)],
                            dest.at[piece],
                            sem_ref.at[len(copies)],
                        )
                    )
                    copies[-1].start()
        targ_ref[...] += jnp.dot(tbf_ref[...], proto_t, preferred_element_type=F32)
        weight = jnp.dot(cols_ref[...], grad_ref[...], preferred_element_type=F32)
        curvature = jnp.sum(proto_bf.astype(F32) * weight, axis=0, keepdims=True)
        weight_ref[...] = inverse * (weight - unit * curvature)
        for position, j in enumerate(order):
            start = pl.multiple_of((place_ref[1] ^ j) * block_rows, block_rows)
            dest, index = (keep_ref, position) if position < blocks // 2 else (send_ref, position - blocks // 2)
            dest[index * block_rows : (index + 1) * block_rows] = weight_ref[pl.ds(start, block_rows)]

        if last:
            total = jnp.zeros((images, dim), F32)
            for group in range(groups):
                base = group * part_rows
                tbase = group * 2 * images
                crop_rows = [
                    rows_ref[base + c * images : base + (c + 1) * images].astype(F32) for c in range(crops)
                ]
                shared = crop_rows[2]
                for c in range(3, crops):
                    shared = shared + crop_rows[c]
                total = total + targ_ref[tbase : tbase + images] * (crop_rows[1] + shared)
                total = total + targ_ref[tbase + images : tbase + 2 * images] * (crop_rows[0] + shared)
            product = jnp.sum(jnp.sum(total, axis=0, keepdims=True), axis=1, keepdims=True)
            loss = norm_ref[:, :1] * (1.0 / (4 * pieces)) - product * (1.0 / (factor * STUDENT_TEMP))
            keep_ref[half:] = loss + jnp.zeros((LOSS_ROWS, width), F32)
            send_ref[half:] = loss + jnp.zeros((LOSS_ROWS, width), F32)
            for copy in copies:
                copy.wait()

    out_shape = [hbm((out_rows, steps * width), F32)] * 2
    out_specs = [pl.BlockSpec((out_rows, width), lambda i, s: (0, i))] * 2
    operands = [protos, mass, column_sums, row_sum, rows, cols, offsets]
    in_specs = [
        pl.BlockSpec((dim, width), lambda i, s: (0, s[0] * total_steps + s[3] + i)),
    ] + [WHOLE] * 6
    aliases = {}
    scratch = []
    if last:
        operands.append(norm_sum)
        in_specs.append(WHOLE)
    if not first:
        operands += list(carried)
        in_specs += [WHOLE] * 2
    if last:
        shape = (pieces, crops, piece_images, dim)
        out_shape = out_shape + [hbm(shape, F32)] * 4
        out_specs = out_specs + [pl.BlockSpec(memory_space=pl.ANY)] * 4
    else:
        out_shape = out_shape + [vmem((groups, crops, images, dim), F32), vmem((teacher_rows, dim), F32)]
        out_specs = out_specs + [WHOLE] * 2
        if not first:
            aliases = {8: 2, 9: 3}
    scratch += [
        pltpu.VMEM((row_count, width), BF16),
        pltpu.VMEM((teacher_rows, width), BF16),
        pltpu.VMEM((teacher_rows, 128), F32),
        pltpu.VMEM((dim, width), F32),
        pltpu.VMEM((part_rows, width), F32),
        pltpu.VMEM((part_rows, width), F32),
    ]
    if last:
        assert steps == 1 and not first
        scratch.append(pltpu.SemaphoreType.DMA((4 * pieces,)))
    return pl.pallas_call(
        kernel,
        grid_spec=pltpu.PrefetchScalarGridSpec(
            num_scalar_prefetch=1, grid=(steps,), in_specs=in_specs, out_specs=out_specs, scratch_shapes=scratch
        ),
        out_shape=out_shape,
        input_output_aliases=aliases,
        compiler_params=params(),
        cost_estimate=cost(10),
        name="gradients",
    )(place, *operands)


def assemble(place, pieces, first, base):
    rows = pieces[0][0].shape[0]
    count = 4 * len(pieces)
    quarter = sum(CHUNKS)
    unit = pieces[0][0].shape[1] // CHUNKS[first]
    columns = 4 * quarter * unit
    flat = [piece for chunk in pieces for piece in chunk]

    def kernel(place_ref, *refs):
        out_ref, sem_ref = refs[-2:]
        copies = []
        for chunk in range(len(pieces)):
            width = CHUNKS[first + chunk] * unit
            offset = sum(CHUNKS[: first + chunk]) * unit
            for j in range(4):
                at = pl.multiple_of((place_ref[0] ^ j) * (quarter * unit) + offset, 128)
                index = 4 * chunk + j
                copies.append(
                    pltpu.make_async_copy(refs[index], out_ref.at[:, pl.ds(at, width)], sem_ref.at[index])
                )
                copies[-1].start()
        for copy in copies:
            copy.wait()

    anywhere = pl.BlockSpec(memory_space=pl.ANY)
    operands = flat if base is None else flat + [base]
    return pl.pallas_call(
        kernel,
        in_specs=[SCALARS] + [anywhere] * len(operands),
        out_specs=anywhere,
        out_shape=jax.ShapeDtypeStruct((rows, columns), F32),
        scratch_shapes=[pltpu.SemaphoreType.DMA((count,))],
        input_output_aliases={} if base is None else {1 + count: 0},
        compiler_params=params(),
        cost_estimate=cost(1.5),
        name="assemble",
    )(place, *operands)


def finish(near, received, unit, raw):
    shape = near.shape
    rows = [value.reshape(-1, shape[-1]) for value in (near, received, unit, raw)]

    def kernel(near_ref, received_ref, unit_ref, raw_ref, out_ref):
        cotangent = near_ref[...] + received_ref[...]
        unit = unit_ref[...]
        floats = raw_ref[...].astype(F32)
        scale = lax.rsqrt(jnp.sum(floats * floats, axis=1, keepdims=True) + NORM_EPS)
        out_ref[...] = scale * (cotangent - unit * jnp.sum(unit * cotangent, axis=1, keepdims=True))

    return pl.pallas_call(
        kernel,
        in_specs=[WHOLE] * 4,
        out_specs=WHOLE,
        out_shape=jax.ShapeDtypeStruct(rows[0].shape, F32),
        compiler_params=params(),
        cost_estimate=cost(1),
        name="finish",
    )(*rows).reshape(shape)


def step_on_device(student_features, teacher_features, student_prototypes, teacher_prototypes):
    student_prototypes = pltpu.with_memory_space_constraint(student_prototypes, pltpu.HBM)
    teacher_prototypes = pltpu.with_memory_space_constraint(teacher_prototypes, pltpu.HBM)
    crops, images, dim = student_features.shape
    proto_local = student_prototypes.shape[1]
    batch_devices = lax.axis_size(BATCH)
    proto_devices = lax.axis_size(PROTO)
    batch_bits = bits_of(batch_devices)
    proto_bits = bits_of(proto_devices)
    images_all = images * batch_devices
    sample_number = teacher_features.shape[0] * images_all
    factor = 1.0 / (images_all * PAIRS * STUDENT_TEMP)
    batch_index = lax.axis_index(BATCH)
    proto_index = lax.axis_index(PROTO)
    core, top = 0, batch_bits - 1
    middle = list(range(1, top))
    place = ((batch_index >> top) & 1) * 2 + (batch_index & 1)
    own_images = images // proto_devices
    columns = proto_local // 4
    places = jnp.stack([place, batch_index, proto_index]).astype(jnp.int32)
    chunk_places = [
        jnp.stack([place, batch_index, proto_index, jnp.int32(sum(CHUNKS[:chunk]))]).astype(jnp.int32)
        for chunk in range(len(CHUNKS))
    ]
    row_places = jnp.stack([place, proto_index]).astype(jnp.int32)

    teacher_own = unit_values(teacher_features.reshape(-1, dim))
    teacher_core = swap(teacher_own, BATCH, core)
    teacher_far = swap(teacher_own, BATCH, top)
    teacher_far_core = swap(teacher_far, BATCH, core)

    own_rows = unit_values(student_features.reshape(-1, dim))
    all_sums = row_sums(places, own_rows, student_prototypes, min(1024, proto_local))

    mass, column_sum = teacher_mass(
        places,
        [teacher_own, teacher_core, teacher_far, teacher_far_core],
        teacher_prototypes,
        columns,
        min(1024, columns),
    )

    own_start = proto_index * own_images
    unit_own = lax.dynamic_slice_in_dim(own_rows.reshape(crops, images, dim), own_start, own_images, 1)
    raw_own = lax.dynamic_slice_in_dim(student_features, own_start, own_images, 1)
    far = swap(unit_own, BATCH, top)[None]
    for bit in range(proto_bits):
        received = swap(far, PROTO, bit)
        far = jnp.concatenate([far, received], axis=0)
    core_rows = swap(own_rows, BATCH, core)
    far_core = swap(far, BATCH, core)
    rows, cols = gather_rows(row_places, own_rows, core_rows, far, far_core, crops, images)

    row_parts = None
    for sweep_index in range(SK_ITERS):
        if sweep_index:
            column_sum = column_pass(row_parts, mass, sample_number)
        for bit in middle[:-1]:
            column_sum = column_sum + swap(column_sum, BATCH, bit)
        column_parts = (column_sum, swap(column_sum, BATCH, middle[-1]))
        row_sum = row_pass(column_parts, mass, None if sweep_index else all_sums)
        row_sum = bits_sum(row_sum, PROTO, range(proto_bits))
        received = swap(row_sum, BATCH, top)
        row_sum = row_sum + received
        row_parts = (row_sum, swap(row_sum, BATCH, core))
        if sweep_index == 0:
            offsets, norm_sum = row_offsets(row_parts, mass.shape[0], crops, images, factor)

    row_total = row_parts[0] + row_parts[1]
    column_total = column_parts[0] + column_parts[1]
    order = [0]
    for bit in [core, top] + middle[::-1]:
        order = order + [j | (1 << bit) for j in order]
    geometry = (crops, images, proto_devices, batch_devices, factor, order)
    carried = None
    pieces = []
    for chunk, steps in enumerate(CHUNKS):
        outs = gradients(
            chunk_places[chunk], steps, chunk == 0, chunk == len(CHUNKS) - 1, student_prototypes, mass,
            column_total, row_total, rows, cols, offsets, norm_sum, carried, geometry,
        )
        send, keep = outs[:2]
        carried = outs[2:]
        loss_rows = LOSS_ROWS if chunk == len(CHUNKS) - 1 else 0
        for bit in middle[:-1]:
            keep = keep + swap(send, BATCH, bit)
            end = keep.shape[0] - loss_rows
            send = keep[end // 2 :]
            keep = jnp.concatenate([keep[: end // 2], keep[end:]], axis=0)
        half = (keep.shape[0] - loss_rows) // 2
        quarter = half // 2
        received = swap(send, BATCH, middle[-1])
        far_send = keep[half:] + received[half:]
        near_own = keep[:quarter] + received[:quarter]
        near_core = keep[quarter:half] + received[quarter:half]
        far_half = swap(far_send, BATCH, top)
        near_core = swap(near_core, BATCH, core)
        far_core = far_half[quarter:half]
        if loss_rows:
            loss = far_send[half:] + far_half[half:]
            far_core = jnp.concatenate([far_core, loss], axis=0)
        far_core = swap(far_core, BATCH, core)
        if loss_rows:
            loss = (loss + far_core[quarter:])[:1, :128]
        pieces.append([near_own, near_core, far_half[:quarter], far_core[:quarter]])
    early = len(CHUNKS) - 2
    grad_prototypes = assemble(places, pieces[:early], 0, None)
    grad_prototypes = assemble(places, pieces[early:], early, grad_prototypes)

    far_wings, near_wings = carried[:2], carried[2:]
    received = [swap(far_wings[1], BATCH, core)]
    received = [swap(far_wings[0], BATCH, core)] + received
    totals = []
    for wing in range(2):
        part = (near_wings[wing] + received[wing]).reshape((2,) * proto_bits + (crops, own_images, dim))
        axes = list(range(proto_bits))
        axes = axes[wing % proto_bits :] + axes[: wing % proto_bits]
        for axis in axes:
            bit = proto_bits - 1 - axis
            near = lax.slice_in_dim(part, 0, 1, axis=axis)
            away = lax.slice_in_dim(part, 1, 2, axis=axis)
            part = near + swap(away, PROTO, bit)
        totals.append(part.reshape(crops, own_images, dim))
    received = swap(totals[1], BATCH, top)
    grad_features = finish(totals[0], received, unit_own, raw_own)

    loss = bits_sum(loss, PROTO, range(proto_bits))
    mean_loss = loss[0, 0] / (images_all * PAIRS)
    return (mean_loss, grad_features, grad_prototypes)


def solution(mesh):
    placed = (P(None, BATCH, None), P(None, BATCH, None), P(None, PROTO), P(None, PROTO))
    return jax.shard_map(
        step_on_device,
        mesh=mesh,
        in_specs=placed,
        out_specs=(P(), P(None, (BATCH, PROTO), None), P(BATCH, PROTO)),
        check_vma=False,
    )
```

```python
import math

import jax
import jax.numpy as jnp
from jax import lax
from jax.experimental import pallas as pl
from jax.experimental.pallas import tpu as pltpu
from jax.sharding import PartitionSpec as P


CLUSTER_NUMBER = 65536
SK_ITERS = 3
BATCH = "batch"
PROTO = "proto"
PAIRS = 18

STUDENT_TEMP = 0.1
TEACHER_TEMP = 0.07
NORM_EPS = 1e-06
LOG2E = math.log2(math.e)

CHUNKS = (1, 2, 2, 2, 1)
LOSS_ROWS = 8
MIB = 1 << 20
F32 = jnp.float32
BF16 = jnp.bfloat16
WHOLE = pl.BlockSpec(memory_space=pltpu.VMEM)
SCALARS = pl.BlockSpec(memory_space=pltpu.SMEM)


def vmem(shape, dtype):
    return pltpu.VMEM(shape, dtype)


def hbm(shape, dtype):
    return pltpu.HBM(shape, dtype)


def params():
    return pltpu.CompilerParams(vmem_limit_bytes=16 * MIB)


def cost(micros):
    return pl.CostEstimate(flops=int(micros * 1e9), transcendentals=0, bytes_accessed=int(micros * 1e6))


def exchange(value, axis, mask):
    size = lax.axis_size(axis)
    return lax.ppermute(value, axis, [(i, i ^ mask) for i in range(size)])


def swap(value, axis, bit):
    return exchange(value, axis, 1 << bit)


def bits_sum(value, axis, bits):
    for first in range(0, len(bits), 2):
        masks = [0]
        for bit in bits[first : first + 2]:
            masks += [mask | (1 << bit) for mask in masks]
        received = []
        for mask in masks[1:]:
            received.append(exchange(value, axis, mask))
        for part in received:
            value = value + part
    return value


def bits_of(size):
    return size.bit_length() - 1


def unit_values(values):
    def kernel(in_ref, out_ref):
        floats = in_ref[...].astype(F32)
        out_ref[...] = floats * lax.rsqrt(jnp.sum(floats * floats, axis=1, keepdims=True) + NORM_EPS)

    return pl.pallas_call(
        kernel,
        in_specs=[WHOLE],
        out_specs=WHOLE,
        out_shape=jax.ShapeDtypeStruct(values.shape, F32),
        compiler_params=params(),
        cost_estimate=cost(1),
        name="units",
    )(values)


def column_scale(floats):
    return lax.rsqrt(jnp.sum(floats * floats, axis=0, keepdims=True) + NORM_EPS)


def rows_to_lanes(partial):
    return jnp.concatenate(
        [
            jnp.sum(partial[i : i + 128].T, axis=0, keepdims=True)
            for i in range(0, partial.shape[0], 128)
        ],
        axis=1,
    )


def lanes_to_rows(values, start):
    return jnp.broadcast_to(values[:, start : start + 128], (128, 128)).T


def row_sums(place, unit, protos, width):
    rows, dim = unit.shape
    columns = protos.shape[1]
    steps = columns // width

    def kernel(place_ref, unit_ref, proto_ref, out_ref, rows_ref, sum_ref):
        step = pl.program_id(0)

        @pl.when(step == 0)
        def _():
            rows_ref[...] = unit_ref[...].astype(BF16)
            sum_ref[...] = jnp.zeros_like(sum_ref)

        for start in range(0, width, 512):
            floats = proto_ref[:, start : start + 512].astype(F32)
            proto_bf = (floats * column_scale(floats)).astype(BF16)
            cos = jnp.dot(rows_ref[...], proto_bf, preferred_element_type=F32)
            mass = jnp.exp2(cos * (LOG2E / STUDENT_TEMP))
            total = mass[:, :128]
            for lane in range(128, 512, 128):
                total = total + mass[:, lane : lane + 128]
            sum_ref[...] += total

        @pl.when(step == steps - 1)
        def _():
            out_ref[...] = jnp.zeros_like(out_ref)
            start = pl.multiple_of(place_ref[0] * rows, rows)
            out_ref[:, pl.ds(start, rows)] = rows_to_lanes(sum_ref[...])

    return pl.pallas_call(
        kernel,
        grid=(steps,),
        in_specs=[
            SCALARS,
            pl.BlockSpec((rows, dim), lambda i: (0, 0)),
            pl.BlockSpec((dim, width), lambda i: (0, i)),
        ],
        out_specs=pl.BlockSpec((1, 4 * rows), lambda i: (0, 0)),
        out_shape=jax.ShapeDtypeStruct((1, 4 * rows), F32),
        scratch_shapes=[pltpu.VMEM((rows, dim), BF16), pltpu.VMEM((rows, 128), F32)],
        compiler_params=params(),
        cost_estimate=cost(15),
        name="row_sums",
    )(place, unit, protos)


def teacher_mass(place, gathered, protos, columns, width):
    part_rows, dim = gathered[0].shape
    rows = part_rows * len(gathered)
    steps = columns // width

    def kernel(place_ref, *refs):
        parts = refs[: len(gathered)]
        proto_ref, mass_ref, sum_ref, rows_ref = refs[len(gathered) :]
        step = pl.program_id(0)

        @pl.when(step == 0)
        def _():
            for j, part in enumerate(parts):
                start = pl.multiple_of((place_ref[0] ^ j) * part_rows, part_rows)
                rows_ref[pl.ds(start, part_rows)] = part[...].astype(BF16)

        at = pl.multiple_of(step * width, width)
        part = min(512, width)
        for start in range(0, width, part):
            floats = proto_ref[:, start : start + part].astype(F32)
            proto_bf = (floats * column_scale(floats)).astype(BF16)
            cos = jnp.dot(rows_ref[...], proto_bf, preferred_element_type=F32)
            mass = jnp.exp2(cos * (LOG2E / TEACHER_TEMP))
            mass_ref[:, pl.ds(at + start, part)] = mass
            sum_ref[:, start : start + part] = jnp.sum(mass, axis=0, keepdims=True)

    return pl.pallas_call(
        kernel,
        grid_spec=pltpu.PrefetchScalarGridSpec(
            num_scalar_prefetch=1,
            grid=(steps,),
            in_specs=[pl.BlockSpec((part_rows, dim), lambda i, s: (0, 0)) for _ in gathered]
            + [pl.BlockSpec((dim, width), lambda i, s: (0, s[0] * steps + i))],
            out_specs=[WHOLE, pl.BlockSpec((1, width), lambda i, s: (0, i))],
            scratch_shapes=[pltpu.VMEM((rows, dim), BF16)],
        ),
        out_shape=[vmem((rows, columns), F32), jax.ShapeDtypeStruct((1, columns), F32)],
        compiler_params=params(),
        cost_estimate=cost(5),
        name="teacher_mass",
    )(place, *gathered, protos)


def row_pass(column_parts, mass, extra):
    rows, columns = mass.shape
    extras = [] if extra is None else [extra]
    total_rows = rows + sum(part.shape[1] for part in extras)

    def kernel(a_ref, b_ref, mass_ref, *refs):
        out_ref = refs[-1]
        scale = 1.0 / (CLUSTER_NUMBER * (a_ref[...] + b_ref[...]))

        def block(index, carry):
            start = pl.multiple_of(index * 128, 128)
            total = jnp.zeros((128, 128), F32)
            for lane in range(0, columns, 128):
                total = total + (
                    mass_ref[pl.ds(start, 128), lane : lane + 128] * scale[:, lane : lane + 128]
                )
            out_ref[:, pl.ds(start, 128)] = jnp.sum(total.T, axis=0, keepdims=True)
            return carry

        lax.fori_loop(0, rows // 128, block, 0, unroll=2)
        if extras:
            out_ref[:, rows:] = refs[0][...]

    return pl.pallas_call(
        kernel,
        in_specs=[WHOLE] * (3 + len(extras)),
        out_specs=WHOLE,
        out_shape=jax.ShapeDtypeStruct((1, total_rows), F32),
        compiler_params=params(),
        cost_estimate=cost(1.5),
        name="row_pass",
    )(*column_parts, mass, *extras)


def column_pass(row_parts, mass, sample_number):
    rows, columns = mass.shape

    def kernel(a_ref, b_ref, mass_ref, out_ref, scale_ref):
        scale = 1.0 / (sample_number * (a_ref[:, :rows] + b_ref[:, :rows]))
        for start in range(0, rows, 128):
            scale_ref[start : start + 128] = lanes_to_rows(scale, start)

        def block(index, carry):
            lane = pl.multiple_of(index * 256, 256)
            total = jnp.zeros((8, 256), F32)
            for start in range(0, rows, 128):
                scales = jnp.concatenate([scale_ref[start : start + 128]] * 2, axis=1)
                term = mass_ref[start : start + 128, pl.ds(lane, 256)] * scales
                total = total + jnp.sum(term.reshape(16, 8, 256), axis=0)
            out_ref[:, pl.ds(lane, 256)] = jnp.sum(total, axis=0, keepdims=True)
            return carry

        lax.fori_loop(0, columns // 256, block, 0, unroll=2)

    return pl.pallas_call(
        kernel,
        in_specs=[WHOLE] * 3,
        out_specs=WHOLE,
        out_shape=jax.ShapeDtypeStruct((1, columns), F32),
        scratch_shapes=[pltpu.VMEM((rows, 128), F32)],
        compiler_params=params(),
        cost_estimate=cost(1.5),
        name="column_pass",
    )(*row_parts, mass)


def gather_rows(place, own, core, far, far_core, crops, images):
    dim = own.shape[1]
    part_rows = crops * images
    pieces, _, piece_images, _ = far.shape
    rows = 4 * part_rows

    def kernel(place_ref, own_ref, core_ref, far_ref, far_core_ref, rows_ref, cols_ref, work_ref):
        def store(j, values):
            start = pl.multiple_of((place_ref[0] ^ j) * part_rows, part_rows)
            rows_ref[pl.ds(start, part_rows)] = values.astype(BF16)
            cols_ref[:, pl.ds(start, part_rows)] = values.T.astype(BF16)

        store(0, own_ref[...])
        store(1, core_ref[...])
        for j, ref in ((2, far_ref), (3, far_core_ref)):

            def move(crop, carry, ref=ref):
                for piece in range(pieces):
                    offset = (place_ref[1] ^ piece) * piece_images
                    at = pl.multiple_of(crop * images + offset, piece_images)
                    work_ref[pl.ds(at, piece_images)] = ref[piece, crop]
                return carry

            lax.fori_loop(0, crops, move, 0)
            store(j, work_ref[...])

    return pl.pallas_call(
        kernel,
        in_specs=[SCALARS] + [WHOLE] * 4,
        out_specs=[WHOLE] * 2,
        out_shape=[vmem((rows, dim), BF16), vmem((dim, rows), BF16)],
        scratch_shapes=[pltpu.VMEM((part_rows, dim), F32)],
        compiler_params=params(),
        cost_estimate=cost(3),
        name="gather_rows",
    )(place, own, core, far, far_core)


def row_offsets(parts, skip, crops, images, factor):
    rows = parts[0].shape[1] - skip

    def kernel(a_ref, b_ref, out_ref, norm_ref, sums_ref):
        sums_ref[...] = a_ref[:, skip:] + b_ref[:, skip:]

        def block(index, total):
            start = pl.multiple_of(index * 128, 128)
            pair_count = jnp.where((start // images) % crops < 2, F32(1.0), F32(2.0))
            sums = sums_ref[:, pl.ds(start, 128)]
            out_ref[pl.ds(start, 128)] = lanes_to_rows(jnp.log2((pair_count * factor) / sums), 0)
            return total + pair_count * jnp.log(sums)

        total = lax.fori_loop(0, rows // 128, block, jnp.zeros((1, 128), F32), unroll=10)
        norm_ref[...] = jnp.sum(total, axis=1, keepdims=True) + jnp.zeros((1, 128), F32)

    return pl.pallas_call(
        kernel,
        in_specs=[WHOLE] * 2,
        out_specs=[WHOLE] * 2,
        out_shape=[vmem((rows, 128), F32), jax.ShapeDtypeStruct((1, 128), F32)],
        scratch_shapes=[pltpu.VMEM((1, rows), F32)],
        compiler_params=params(),
        cost_estimate=cost(1),
        name="row_offsets",
    )(*parts)


def gradients(place, steps, first, last, protos, mass, column_sums, row_sum, rows, cols, offsets, norm_sum, carried, geometry):
    crops, images, pieces, blocks, factor, order = geometry
    dim = protos.shape[0]
    half = dim // 2
    out_rows = half + (LOSS_ROWS if last else 0)
    row_count = rows.shape[0]
    teacher_rows, columns = mass.shape
    groups = teacher_rows // (2 * images)
    part_rows = crops * images
    piece_images = images // pieces
    total_steps = sum(CHUNKS)
    width = columns // total_steps
    block_rows = dim // blocks

    def kernel(place_ref, *refs):
        refs = list(refs)
        proto_ref, mass_ref, csum_ref, rsum_ref, rows_ref, cols_ref, offs_ref = refs[:7]
        refs = refs[7:]
        if last:
            norm_ref = refs.pop(0)
        if not first:
            feat_in, targ_in = refs[:2]
            refs = refs[2:]
        send_ref, keep_ref = refs[:2]
        refs = refs[2:]
        if last:
            wing_refs = refs[:4]
            refs = refs[4:]
            sem_ref = refs.pop()
            feat_ref, targ_ref = feat_in, targ_in
        else:
            feat_ref, targ_ref = refs[:2]
            refs = refs[2:]
        grad_ref, tbf_ref, rscale_ref, weight_ref, *cos_refs = refs
        step = pl.program_id(0)

        @pl.when(step == 0)
        def _():
            scale = factor / rsum_ref[...]
            for start in range(0, teacher_rows, 128):
                rscale_ref[start : start + 128] = lanes_to_rows(scale, start)
            if first:

                def clear(crop, carry):
                    feat_ref[:, pl.ds(crop, 1)] = jnp.zeros((groups, 1, images, dim), F32)
                    return carry

                lax.fori_loop(0, crops, clear, 0)
                targ_ref[...] = jnp.zeros_like(targ_ref)

        at = pl.multiple_of((place_ref[3] + step) * width, width)
        floats = proto_ref[...].astype(F32)
        inverse = column_scale(floats)
        unit = floats * inverse
        proto_bf = unit.astype(BF16)
        proto_t = unit.T.astype(BF16)
        cscale = 1.0 / (CLUSTER_NUMBER * csum_ref[:, pl.ds(at, width)])

        for group in range(groups):
            base = group * part_rows
            tbase = group * 2 * images
            cos_ref = cos_refs[group % 2]
            cos_ref[...] = jnp.dot(rows_ref[base : base + part_rows], proto_bf, preferred_element_type=F32)
            for lane in range(0, width, 128):
                lanes = slice(lane, lane + 128)
                for image in range(0, images, 64):
                    pair = []
                    for wide in range(2):
                        start = tbase + wide * images + image
                        target = (
                            mass_ref[start : start + 64, pl.ds(at + lane, 128)]
                            * rscale_ref[start : start + 64]
                            * cscale[:, lanes]
                        )
                        tbf_ref[start : start + 64, lanes] = target.astype(BF16)
                        pair.append(target)
                    both = pair[0] + pair[1]
                    for crop in range(crops):
                        start = crop * images + image
                        power = cos_ref[start : start + 64, lanes] * (LOG2E / STUDENT_TEMP)
                        prob = jnp.exp2(power + offs_ref[base + start : base + start + 64])
                        target = pair[1] if crop == 0 else pair[0] if crop == 1 else both
                        grad_ref[base + start : base + start + 64, lanes] = (prob - target).astype(BF16)
            product = jnp.dot(grad_ref[base : base + part_rows], proto_t, preferred_element_type=F32)
            feat_ref[group] += product.reshape(crops, images, dim)
        copies = []
        if last:
            for j in range(4):
                dest = wing_refs[(j >> 1) + (0 if j & 1 else 2)]
                for piece in range(pieces):
                    start = pl.multiple_of((place_ref[2] ^ piece) * piece_images, piece_images)
                    copies.append(
                        pltpu.make_async_copy(
                            feat_ref.at[place_ref[0] ^ j, :, pl.ds(start, piece_images)],
                            dest.at[piece],
                            sem_ref.at[len(copies)],
                        )
                    )
                    copies[-1].start()
        targ_ref[...] += jnp.dot(tbf_ref[...], proto_t, preferred_element_type=F32)
        weight_ref[...] = jnp.zeros_like(weight_ref)

        def part_of_rows(index, carry):
            part = pl.ds(pl.multiple_of(index * (row_count // 2), row_count // 2), row_count // 2)
            weight_ref[...] += jnp.dot(cols_ref[:, part], grad_ref[part], preferred_element_type=F32)
            return carry

        lax.fori_loop(0, 2, part_of_rows, 0)
        weight = weight_ref[...]
        curvature = jnp.sum(proto_bf.astype(F32) * weight, axis=0, keepdims=True)
        weight_ref[...] = inverse * (weight - unit * curvature)
        for position, j in enumerate(order):
            start = pl.multiple_of((place_ref[1] ^ j) * block_rows, block_rows)
            dest, index = (keep_ref, position) if position < blocks // 2 else (send_ref, position - blocks // 2)
            dest[index * block_rows : (index + 1) * block_rows] = weight_ref[pl.ds(start, block_rows)]

        if last:
            total = jnp.zeros((images, dim), F32)
            for group in range(groups):
                base = group * part_rows
                tbase = group * 2 * images
                crop_rows = [
                    rows_ref[base + c * images : base + (c + 1) * images].astype(F32) for c in range(crops)
                ]
                shared = crop_rows[2]
                for c in range(3, crops):
                    shared = shared + crop_rows[c]
                total = total + targ_ref[tbase : tbase + images] * (crop_rows[1] + shared)
                total = total + targ_ref[tbase + images : tbase + 2 * images] * (crop_rows[0] + shared)
            product = jnp.sum(jnp.sum(total, axis=0, keepdims=True), axis=1, keepdims=True)
            loss = norm_ref[:, :1] * (1.0 / (4 * pieces)) - product * (1.0 / (factor * STUDENT_TEMP))
            keep_ref[half:] = loss + jnp.zeros((LOSS_ROWS, width), F32)
            send_ref[half:] = loss + jnp.zeros((LOSS_ROWS, width), F32)
            for copy in copies:
                copy.wait()

    out_shape = [hbm((out_rows, steps * width), F32)] * 2
    out_specs = [pl.BlockSpec((out_rows, width), lambda i, s: (0, i))] * 2
    operands = [protos, mass, column_sums, row_sum, rows, cols, offsets]
    in_specs = [
        pl.BlockSpec((dim, width), lambda i, s: (0, s[0] * total_steps + s[3] + i)),
    ] + [WHOLE] * 6
    aliases = {}
    scratch = []
    if last:
        operands.append(norm_sum)
        in_specs.append(WHOLE)
    if not first:
        operands += list(carried)
        in_specs += [WHOLE] * 2
    if last:
        shape = (pieces, crops, piece_images, dim)
        out_shape = out_shape + [hbm(shape, F32)] * 4
        out_specs = out_specs + [pl.BlockSpec(memory_space=pl.ANY)] * 4
    else:
        out_shape = out_shape + [vmem((groups, crops, images, dim), F32), vmem((teacher_rows, dim), F32)]
        out_specs = out_specs + [WHOLE] * 2
        if not first:
            aliases = {8: 2, 9: 3}
    scratch += [
        pltpu.VMEM((row_count, width), BF16),
        pltpu.VMEM((teacher_rows, width), BF16),
        pltpu.VMEM((teacher_rows, 128), F32),
        pltpu.VMEM((dim, width), F32),
        pltpu.VMEM((part_rows, width), F32),
        pltpu.VMEM((part_rows, width), F32),
    ]
    if last:
        assert steps == 1 and not first
        scratch.append(pltpu.SemaphoreType.DMA((4 * pieces,)))
    return pl.pallas_call(
        kernel,
        grid_spec=pltpu.PrefetchScalarGridSpec(
            num_scalar_prefetch=1, grid=(steps,), in_specs=in_specs, out_specs=out_specs, scratch_shapes=scratch
        ),
        out_shape=out_shape,
        input_output_aliases=aliases,
        compiler_params=params(),
        cost_estimate=cost(10),
        name="gradients",
    )(place, *operands)


def assemble(place, pieces, first, base):
    rows = pieces[0][0].shape[0]
    count = 4 * len(pieces)
    quarter = sum(CHUNKS)
    unit = pieces[0][0].shape[1] // CHUNKS[first]
    columns = 4 * quarter * unit
    flat = [piece for chunk in pieces for piece in chunk]

    def kernel(place_ref, *refs):
        out_ref, sem_ref = refs[-2:]
        copies = []
        for chunk in range(len(pieces)):
            width = CHUNKS[first + chunk] * unit
            offset = sum(CHUNKS[: first + chunk]) * unit
            for j in range(4):
                at = pl.multiple_of((place_ref[0] ^ j) * (quarter * unit) + offset, 128)
                index = 4 * chunk + j
                copies.append(
                    pltpu.make_async_copy(refs[index], out_ref.at[:, pl.ds(at, width)], sem_ref.at[index])
                )
                copies[-1].start()
        for copy in copies:
            copy.wait()

    anywhere = pl.BlockSpec(memory_space=pl.ANY)
    operands = flat if base is None else flat + [base]
    return pl.pallas_call(
        kernel,
        in_specs=[SCALARS] + [anywhere] * len(operands),
        out_specs=anywhere,
        out_shape=jax.ShapeDtypeStruct((rows, columns), F32),
        scratch_shapes=[pltpu.SemaphoreType.DMA((count,))],
        input_output_aliases={} if base is None else {1 + count: 0},
        compiler_params=params(),
        cost_estimate=cost(1.5),
        name="assemble",
    )(place, *operands)


def finish(near, received, unit, raw):
    shape = near.shape
    rows = [value.reshape(-1, shape[-1]) for value in (near, received, unit, raw)]

    def kernel(near_ref, received_ref, unit_ref, raw_ref, out_ref):
        cotangent = near_ref[...] + received_ref[...]
        unit = unit_ref[...]
        floats = raw_ref[...].astype(F32)
        scale = lax.rsqrt(jnp.sum(floats * floats, axis=1, keepdims=True) + NORM_EPS)
        out_ref[...] = scale * (cotangent - unit * jnp.sum(unit * cotangent, axis=1, keepdims=True))

    return pl.pallas_call(
        kernel,
        in_specs=[WHOLE] * 4,
        out_specs=WHOLE,
        out_shape=jax.ShapeDtypeStruct(rows[0].shape, F32),
        compiler_params=params(),
        cost_estimate=cost(1),
        name="finish",
    )(*rows).reshape(shape)


def step_on_device(student_features, teacher_features, student_prototypes, teacher_prototypes):
    student_prototypes = pltpu.with_memory_space_constraint(student_prototypes, pltpu.HBM)
    teacher_prototypes = pltpu.with_memory_space_constraint(teacher_prototypes, pltpu.HBM)
    crops, images, dim = student_features.shape
    proto_local = student_prototypes.shape[1]
    batch_devices = lax.axis_size(BATCH)
    proto_devices = lax.axis_size(PROTO)
    batch_bits = bits_of(batch_devices)
    proto_bits = bits_of(proto_devices)
    images_all = images * batch_devices
    sample_number = teacher_features.shape[0] * images_all
    factor = 1.0 / (images_all * PAIRS * STUDENT_TEMP)
    batch_index = lax.axis_index(BATCH)
    proto_index = lax.axis_index(PROTO)
    core, top = 0, batch_bits - 1
    middle = list(range(1, top))
    place = ((batch_index >> top) & 1) * 2 + (batch_index & 1)
    own_images = images // proto_devices
    columns = proto_local // 4
    places = jnp.stack([place, batch_index, proto_index]).astype(jnp.int32)
    chunk_places = [
        jnp.stack([place, batch_index, proto_index, jnp.int32(sum(CHUNKS[:chunk]))]).astype(jnp.int32)
        for chunk in range(len(CHUNKS))
    ]
    row_places = jnp.stack([place, proto_index]).astype(jnp.int32)

    teacher_own = unit_values(teacher_features.reshape(-1, dim))
    teacher_core = swap(teacher_own, BATCH, core)
    teacher_far = swap(teacher_own, BATCH, top)
    teacher_far_core = swap(teacher_far, BATCH, core)

    own_rows = unit_values(student_features.reshape(-1, dim))
    all_sums = row_sums(places, own_rows, student_prototypes, min(1024, proto_local))

    mass, column_sum = teacher_mass(
        places,
        [teacher_own, teacher_core, teacher_far, teacher_far_core],
        teacher_prototypes,
        columns,
        min(1024, columns),
    )

    own_start = proto_index * own_images
    unit_own = lax.dynamic_slice_in_dim(own_rows.reshape(crops, images, dim), own_start, own_images, 1)
    raw_own = lax.dynamic_slice_in_dim(student_features, own_start, own_images, 1)
    far = swap(unit_own, BATCH, top)[None]
    for bit in range(proto_bits):
        received = swap(far, PROTO, bit)
        far = jnp.concatenate([far, received], axis=0)
    core_rows = swap(own_rows, BATCH, core)
    far_core = swap(far, BATCH, core)
    rows, cols = gather_rows(row_places, own_rows, core_rows, far, far_core, crops, images)

    row_parts = None
    for sweep_index in range(SK_ITERS):
        if sweep_index:
            column_sum = column_pass(row_parts, mass, sample_number)
        for bit in middle[:-1]:
            column_sum = column_sum + swap(column_sum, BATCH, bit)
        column_parts = (column_sum, swap(column_sum, BATCH, middle[-1]))
        row_sum = row_pass(column_parts, mass, None if sweep_index else all_sums)
        row_sum = bits_sum(row_sum, PROTO, range(proto_bits))
        received = swap(row_sum, BATCH, top)
        row_sum = row_sum + received
        row_parts = (row_sum, swap(row_sum, BATCH, core))
        if sweep_index == 0:
            offsets, norm_sum = row_offsets(row_parts, mass.shape[0], crops, images, factor)

    row_total = row_parts[0] + row_parts[1]
    column_total = column_parts[0] + column_parts[1]
    order = [0]
    for bit in [core, top] + middle[::-1]:
        order = order + [j | (1 << bit) for j in order]
    geometry = (crops, images, proto_devices, batch_devices, factor, order)
    carried = None
    pieces = []
    for chunk, steps in enumerate(CHUNKS):
        outs = gradients(
            chunk_places[chunk], steps, chunk == 0, chunk == len(CHUNKS) - 1, student_prototypes, mass,
            column_total, row_total, rows, cols, offsets, norm_sum, carried, geometry,
        )
        send, keep = outs[:2]
        carried = outs[2:]
        loss_rows = LOSS_ROWS if chunk == len(CHUNKS) - 1 else 0
        for bit in middle[:-1]:
            keep = keep + swap(send, BATCH, bit)
            end = keep.shape[0] - loss_rows
            send = keep[end // 2 :]
            keep = jnp.concatenate([keep[: end // 2], keep[end:]], axis=0)
        half = (keep.shape[0] - loss_rows) // 2
        quarter = half // 2
        received = swap(send, BATCH, middle[-1])
        far_send = keep[half:] + received[half:]
        near_own = keep[:quarter] + received[:quarter]
        near_core = keep[quarter:half] + received[quarter:half]
        far_half = swap(far_send, BATCH, top)
        near_core = swap(near_core, BATCH, core)
        far_core = far_half[quarter:half]
        if loss_rows:
            loss = far_send[half:] + far_half[half:]
            far_core = jnp.concatenate([far_core, loss], axis=0)
        far_core = swap(far_core, BATCH, core)
        if loss_rows:
            loss = (loss + far_core[quarter:])[:1, :128]
        pieces.append([near_own, near_core, far_half[:quarter], far_core[:quarter]])
    early = len(CHUNKS) - 2
    grad_prototypes = assemble(places, pieces[:early], 0, None)
    grad_prototypes = assemble(places, pieces[early:], early, grad_prototypes)

    far_wings, near_wings = carried[:2], carried[2:]
    received = [swap(far_wings[1], BATCH, core)]
    received = [swap(far_wings[0], BATCH, core)] + received
    totals = []
    for wing in range(2):
        part = (near_wings[wing] + received[wing]).reshape((2,) * proto_bits + (crops, own_images, dim))
        axes = list(range(proto_bits))
        axes = axes[wing % proto_bits :] + axes[: wing % proto_bits]
        for axis in axes:
            bit = proto_bits - 1 - axis
            near = lax.slice_in_dim(part, 0, 1, axis=axis)
            away = lax.slice_in_dim(part, 1, 2, axis=axis)
            part = near + swap(away, PROTO, bit)
        totals.append(part.reshape(crops, own_images, dim))
    received = swap(totals[1], BATCH, top)
    grad_features = finish(totals[0], received, unit_own, raw_own)

    loss = bits_sum(loss, PROTO, range(proto_bits))
    mean_loss = loss[0, 0] / (images_all * PAIRS)
    return (mean_loss, grad_features, grad_prototypes)


def solution(mesh):
    placed = (P(None, BATCH, None), P(None, BATCH, None), P(None, PROTO), P(None, PROTO))
    return jax.shard_map(
        step_on_device,
        mesh=mesh,
        in_specs=placed,
        out_specs=(P(), P(None, (BATCH, PROTO), None), P(BATCH, PROTO)),
        check_vma=False,
    )
```

```python
import math

import jax
import jax.numpy as jnp
from jax import lax
from jax.experimental import pallas as pl
from jax.experimental.pallas import tpu as pltpu
from jax.sharding import PartitionSpec as P


CLUSTER_NUMBER = 65536
SK_ITERS = 3
BATCH = "batch"
PROTO = "proto"
PAIRS = 18

STUDENT_TEMP = 0.1
TEACHER_TEMP = 0.07
NORM_EPS = 1e-06
LOG2E = math.log2(math.e)

CHUNKS = (1, 2, 2, 2, 1)
MIB = 1 << 20
F32 = jnp.float32
BF16 = jnp.bfloat16
WHOLE = pl.BlockSpec(memory_space=pltpu.VMEM)
SCALARS = pl.BlockSpec(memory_space=pltpu.SMEM)


def vmem(shape, dtype):
    return pltpu.VMEM(shape, dtype)


def hbm(shape, dtype):
    return pltpu.HBM(shape, dtype)


def params():
    return pltpu.CompilerParams(vmem_limit_bytes=16 * MIB)


def cost(micros):
    return pl.CostEstimate(flops=int(micros * 1e9), transcendentals=0, bytes_accessed=int(micros * 1e6))


def exchange(value, axis, mask):
    size = lax.axis_size(axis)
    return lax.ppermute(value, axis, [(i, i ^ mask) for i in range(size)])


def swap(value, axis, bit):
    return exchange(value, axis, 1 << bit)


def bits_sum(value, axis, bits):
    for first in range(0, len(bits), 2):
        masks = [0]
        for bit in bits[first : first + 2]:
            masks += [mask | (1 << bit) for mask in masks]
        received = []
        for mask in masks[1:]:
            received.append(exchange(value, axis, mask))
        for part in received:
            value = value + part
    return value


def bits_of(size):
    return size.bit_length() - 1


def unit_values(values):
    def kernel(in_ref, out_ref):
        floats = in_ref[...].astype(F32)
        out_ref[...] = floats * lax.rsqrt(jnp.sum(floats * floats, axis=1, keepdims=True) + NORM_EPS)

    return pl.pallas_call(
        kernel,
        in_specs=[WHOLE],
        out_specs=WHOLE,
        out_shape=jax.ShapeDtypeStruct(values.shape, F32),
        compiler_params=params(),
        cost_estimate=cost(1),
        name="units",
    )(values)


def column_scale(floats):
    return lax.rsqrt(jnp.sum(floats * floats, axis=0, keepdims=True) + NORM_EPS)


def rows_to_lanes(partial):
    return jnp.concatenate(
        [
            jnp.sum(partial[i : i + 128].T, axis=0, keepdims=True)
            for i in range(0, partial.shape[0], 128)
        ],
        axis=1,
    )


def lanes_to_rows(values, start):
    return jnp.broadcast_to(values[:, start : start + 128], (128, 128)).T


def row_sums(place, unit, protos, width):
    rows, dim = unit.shape
    columns = protos.shape[1]
    steps = columns // width

    def kernel(place_ref, unit_ref, proto_ref, out_ref, rows_ref, sum_ref):
        step = pl.program_id(0)

        @pl.when(step == 0)
        def _():
            rows_ref[...] = unit_ref[...].astype(BF16)
            sum_ref[...] = jnp.zeros_like(sum_ref)

        for start in range(0, width, 512):
            floats = proto_ref[:, start : start + 512].astype(F32)
            proto_bf = (floats * column_scale(floats)).astype(BF16)
            cos = jnp.dot(rows_ref[...], proto_bf, preferred_element_type=F32)
            mass = jnp.exp2(cos * (LOG2E / STUDENT_TEMP))
            total = mass[:, :128]
            for lane in range(128, 512, 128):
                total = total + mass[:, lane : lane + 128]
            sum_ref[...] += total

        @pl.when(step == steps - 1)
        def _():
            out_ref[...] = jnp.zeros_like(out_ref)
            start = pl.multiple_of(place_ref[0] * rows, rows)
            out_ref[:, pl.ds(start, rows)] = rows_to_lanes(sum_ref[...])

    return pl.pallas_call(
        kernel,
        grid=(steps,),
        in_specs=[
            SCALARS,
            pl.BlockSpec((rows, dim), lambda i: (0, 0)),
            pl.BlockSpec((dim, width), lambda i: (0, i)),
        ],
        out_specs=pl.BlockSpec((1, 4 * rows), lambda i: (0, 0)),
        out_shape=jax.ShapeDtypeStruct((1, 4 * rows), F32),
        scratch_shapes=[pltpu.VMEM((rows, dim), BF16), pltpu.VMEM((rows, 128), F32)],
        compiler_params=params(),
        cost_estimate=cost(15),
        name="row_sums",
    )(place, unit, protos)


def teacher_mass(place, gathered, protos, columns, width):
    part_rows, dim = gathered[0].shape
    rows = part_rows * len(gathered)
    steps = columns // width

    def kernel(place_ref, *refs):
        parts = refs[: len(gathered)]
        proto_ref, mass_ref, sum_ref, rows_ref, parts_ref, sem_ref = refs[len(gathered) :]
        step = pl.program_id(0)

        @pl.when(step == 0)
        def _():
            copies = [
                pltpu.make_async_copy(part, parts_ref.at[j], sem_ref.at[j]) for j, part in enumerate(parts)
            ]
            for copy in copies:
                copy.start()
            for j, copy in enumerate(copies):
                copy.wait()
                start = pl.multiple_of((place_ref[0] ^ j) * part_rows, part_rows)
                rows_ref[pl.ds(start, part_rows)] = parts_ref[j].astype(BF16)

        at = pl.multiple_of(step * width, width)
        part = min(512, width)
        for start in range(0, width, part):
            floats = proto_ref[:, start : start + part].astype(F32)
            proto_bf = (floats * column_scale(floats)).astype(BF16)
            cos = jnp.dot(rows_ref[...], proto_bf, preferred_element_type=F32)
            mass = jnp.exp2(cos * (LOG2E / TEACHER_TEMP))
            mass_ref[:, pl.ds(at + start, part)] = mass
            sum_ref[:, start : start + part] = jnp.sum(mass, axis=0, keepdims=True)

    return pl.pallas_call(
        kernel,
        grid_spec=pltpu.PrefetchScalarGridSpec(
            num_scalar_prefetch=1,
            grid=(steps,),
            in_specs=[pl.BlockSpec(memory_space=pl.ANY)] * len(gathered)
            + [pl.BlockSpec((dim, width), lambda i, s: (0, s[0] * steps + i))],
            out_specs=[WHOLE, pl.BlockSpec((1, width), lambda i, s: (0, i))],
            scratch_shapes=[
                pltpu.VMEM((rows, dim), BF16),
                pltpu.VMEM((len(gathered), part_rows, dim), F32),
                pltpu.SemaphoreType.DMA((len(gathered),)),
            ],
        ),
        out_shape=[vmem((rows, columns), F32), jax.ShapeDtypeStruct((1, columns), F32)],
        compiler_params=params(),
        cost_estimate=cost(5),
        name="teacher_mass",
    )(place, *gathered, protos)


def row_pass(column_parts, mass, extra):
    rows, columns = mass.shape
    extras = [] if extra is None else [extra]
    total_rows = rows + sum(part.shape[1] for part in extras)

    def kernel(a_ref, b_ref, mass_ref, *refs):
        out_ref = refs[-1]
        scale = 1.0 / (CLUSTER_NUMBER * (a_ref[...] + b_ref[...]))

        def block(index, carry):
            start = pl.multiple_of(index * 128, 128)
            total = jnp.zeros((128, 128), F32)
            for lane in range(0, columns, 128):
                total = total + (
                    mass_ref[pl.ds(start, 128), lane : lane + 128] * scale[:, lane : lane + 128]
                )
            out_ref[:, pl.ds(start, 128)] = jnp.sum(total.T, axis=0, keepdims=True)
            return carry

        lax.fori_loop(0, rows // 128, block, 0, unroll=2)
        if extras:
            out_ref[:, rows:] = refs[0][...]

    return pl.pallas_call(
        kernel,
        in_specs=[WHOLE] * (3 + len(extras)),
        out_specs=WHOLE,
        out_shape=jax.ShapeDtypeStruct((1, total_rows), F32),
        compiler_params=params(),
        cost_estimate=cost(1.5),
        name="row_pass",
    )(*column_parts, mass, *extras)


def column_pass(row_parts, mass, sample_number):
    rows, columns = mass.shape

    def kernel(a_ref, b_ref, mass_ref, out_ref, scale_ref):
        scale = 1.0 / (sample_number * (a_ref[:, :rows] + b_ref[:, :rows]))
        for start in range(0, rows, 128):
            scale_ref[start : start + 128] = lanes_to_rows(scale, start)

        def block(index, carry):
            lane = pl.multiple_of(index * 256, 256)
            total = jnp.zeros((8, 256), F32)
            for start in range(0, rows, 128):
                scales = jnp.concatenate([scale_ref[start : start + 128]] * 2, axis=1)
                term = mass_ref[start : start + 128, pl.ds(lane, 256)] * scales
                total = total + jnp.sum(term.reshape(16, 8, 256), axis=0)
            out_ref[:, pl.ds(lane, 256)] = jnp.sum(total, axis=0, keepdims=True)
            return carry

        lax.fori_loop(0, columns // 256, block, 0, unroll=2)

    return pl.pallas_call(
        kernel,
        in_specs=[WHOLE] * 3,
        out_specs=WHOLE,
        out_shape=jax.ShapeDtypeStruct((1, columns), F32),
        scratch_shapes=[pltpu.VMEM((rows, 128), F32)],
        compiler_params=params(),
        cost_estimate=cost(1.5),
        name="column_pass",
    )(*row_parts, mass)


def gather_rows(place, own, core, far, far_core, crops, images):
    dim = own.shape[1]
    part_rows = crops * images
    pieces, _, piece_images, _ = far.shape
    rows = 4 * part_rows

    def kernel(place_ref, own_ref, core_ref, far_ref, far_core_ref, rows_ref, cols_ref, work_ref):
        def store(j, values):
            start = pl.multiple_of((place_ref[0] ^ j) * part_rows, part_rows)
            rows_ref[pl.ds(start, part_rows)] = values.astype(BF16)
            cols_ref[:, pl.ds(start, part_rows)] = values.T.astype(BF16)

        store(0, own_ref[...])
        store(1, core_ref[...])
        for j, ref in ((2, far_ref), (3, far_core_ref)):

            def move(crop, carry, ref=ref):
                for piece in range(pieces):
                    offset = (place_ref[1] ^ piece) * piece_images
                    at = pl.multiple_of(crop * images + offset, piece_images)
                    work_ref[pl.ds(at, piece_images)] = ref[piece, crop]
                return carry

            lax.fori_loop(0, crops, move, 0)
            store(j, work_ref[...])

    return pl.pallas_call(
        kernel,
        in_specs=[SCALARS] + [WHOLE] * 4,
        out_specs=[WHOLE] * 2,
        out_shape=[vmem((rows, dim), BF16), vmem((dim, rows), BF16)],
        scratch_shapes=[pltpu.VMEM((part_rows, dim), F32)],
        compiler_params=params(),
        cost_estimate=cost(3),
        name="gather_rows",
    )(place, own, core, far, far_core)


def row_offsets(parts, skip, crops, images, factor):
    rows = parts[0].shape[1] - skip

    def kernel(a_ref, b_ref, out_ref, norm_ref, sums_ref):
        sums_ref[...] = a_ref[:, skip:] + b_ref[:, skip:]

        def block(index, total):
            start = pl.multiple_of(index * 128, 128)
            pair_count = jnp.where((start // images) % crops < 2, F32(1.0), F32(2.0))
            sums = sums_ref[:, pl.ds(start, 128)]
            out_ref[pl.ds(start, 128)] = lanes_to_rows(jnp.log2((pair_count * factor) / sums), 0)
            return total + pair_count * jnp.log(sums)

        total = lax.fori_loop(0, rows // 128, block, jnp.zeros((1, 128), F32), unroll=10)
        norm_ref[...] = jnp.sum(total, axis=1, keepdims=True) + jnp.zeros((1, 128), F32)

    return pl.pallas_call(
        kernel,
        in_specs=[WHOLE] * 2,
        out_specs=[WHOLE] * 2,
        out_shape=[vmem((rows, 128), F32), jax.ShapeDtypeStruct((1, 128), F32)],
        scratch_shapes=[pltpu.VMEM((1, rows), F32)],
        compiler_params=params(),
        cost_estimate=cost(1),
        name="row_offsets",
    )(*parts)


def gradients(place, steps, first, last, protos, mass, column_sums, row_sum, rows, cols, offsets, norm_sum, carried, geometry):
    crops, images, pieces, blocks, factor, order = geometry
    dim = protos.shape[0]
    half = dim // 2
    row_count = rows.shape[0]
    teacher_rows, columns = mass.shape
    groups = teacher_rows // (2 * images)
    part_rows = crops * images
    piece_images = images // pieces
    total_steps = sum(CHUNKS)
    width = columns // total_steps
    block_rows = dim // blocks

    def kernel(place_ref, *refs):
        refs = list(refs)
        proto_ref, mass_ref, csum_ref, rsum_ref, rows_ref, cols_ref, offs_ref = refs[:7]
        refs = refs[7:]
        if last:
            norm_ref = refs.pop(0)
        if not first:
            feat_in, targ_in = refs[:2]
            refs = refs[2:]
        send_ref, keep_ref = refs[:2]
        refs = refs[2:]
        if last:
            wing_refs, loss_ref = refs[:4], refs[4]
            refs = refs[5:]
            sem_ref = refs.pop()
            feat_ref, targ_ref = feat_in, targ_in
        else:
            feat_ref, targ_ref = refs[:2]
            refs = refs[2:]
        grad_ref, tbf_ref, rscale_ref, weight_ref, *cos_refs = refs
        step = pl.program_id(0)

        @pl.when(step == 0)
        def _():
            scale = factor / rsum_ref[...]
            for start in range(0, teacher_rows, 128):
                rscale_ref[start : start + 128] = lanes_to_rows(scale, start)
            if first:

                def clear(crop, carry):
                    feat_ref[:, pl.ds(crop, 1)] = jnp.zeros((groups, 1, images, dim), F32)
                    return carry

                lax.fori_loop(0, crops, clear, 0)
                targ_ref[...] = jnp.zeros_like(targ_ref)

        at = pl.multiple_of((place_ref[3] + step) * width, width)
        floats = proto_ref[...].astype(F32)
        inverse = column_scale(floats)
        unit = floats * inverse
        proto_bf = unit.astype(BF16)
        proto_t = unit.T.astype(BF16)
        cscale = 1.0 / (CLUSTER_NUMBER * csum_ref[:, pl.ds(at, width)])

        for group in range(groups):
            base = group * part_rows
            tbase = group * 2 * images
            cos_ref = cos_refs[group % 2]
            cos_ref[...] = jnp.dot(rows_ref[base : base + part_rows], proto_bf, preferred_element_type=F32)
            for lane in range(0, width, 128):
                lanes = slice(lane, lane + 128)
                for image in range(0, images, 64):
                    pair = []
                    for wide in range(2):
                        start = tbase + wide * images + image
                        target = (
                            mass_ref[start : start + 64, pl.ds(at + lane, 128)]
                            * rscale_ref[start : start + 64]
                            * cscale[:, lanes]
                        )
                        tbf_ref[start : start + 64, lanes] = target.astype(BF16)
                        pair.append(target)
                    both = pair[0] + pair[1]
                    for crop in range(crops):
                        start = crop * images + image
                        power = cos_ref[start : start + 64, lanes] * (LOG2E / STUDENT_TEMP)
                        prob = jnp.exp2(power + offs_ref[base + start : base + start + 64])
                        target = pair[1] if crop == 0 else pair[0] if crop == 1 else both
                        grad_ref[base + start : base + start + 64, lanes] = (prob - target).astype(BF16)
            product = jnp.dot(grad_ref[base : base + part_rows], proto_t, preferred_element_type=F32)
            feat_ref[group] += product.reshape(crops, images, dim)
        copies = []
        if last:
            for j in range(4):
                dest = wing_refs[(j >> 1) + (0 if j & 1 else 2)]
                for piece in range(pieces):
                    start = pl.multiple_of((place_ref[2] ^ piece) * piece_images, piece_images)
                    copies.append(
                        pltpu.make_async_copy(
                            feat_ref.at[place_ref[0] ^ j, :, pl.ds(start, piece_images)],
                            dest.at[piece],
                            sem_ref.at[len(copies)],
                        )
                    )
                    copies[-1].start()
        targ_ref[...] += jnp.dot(tbf_ref[...], proto_t, preferred_element_type=F32)
        weight_ref[...] = jnp.zeros_like(weight_ref)

        def part_of_rows(index, carry):
            part = pl.ds(pl.multiple_of(index * (row_count // 2), row_count // 2), row_count // 2)
            weight_ref[...] += jnp.dot(cols_ref[:, part], grad_ref[part], preferred_element_type=F32)
            return carry

        lax.fori_loop(0, 2, part_of_rows, 0)
        weight = weight_ref[...]
        curvature = jnp.sum(proto_bf.astype(F32) * weight, axis=0, keepdims=True)
        weight_ref[...] = inverse * (weight - unit * curvature)
        for position, j in enumerate(order):
            start = pl.multiple_of((place_ref[1] ^ j) * block_rows, block_rows)
            dest, index = (keep_ref, position) if position < blocks // 2 else (send_ref, position - blocks // 2)
            dest[index * block_rows : (index + 1) * block_rows] = weight_ref[pl.ds(start, block_rows)]

        if last:
            total = jnp.zeros((images, dim), F32)
            for group in range(groups):
                base = group * part_rows
                tbase = group * 2 * images
                crop_rows = [
                    rows_ref[base + c * images : base + (c + 1) * images].astype(F32) for c in range(crops)
                ]
                shared = crop_rows[2]
                for c in range(3, crops):
                    shared = shared + crop_rows[c]
                total = total + targ_ref[tbase : tbase + images] * (crop_rows[1] + shared)
                total = total + targ_ref[tbase + images : tbase + 2 * images] * (crop_rows[0] + shared)
            product = jnp.sum(jnp.sum(total, axis=0, keepdims=True), axis=1, keepdims=True)
            loss = norm_ref[:, :1] * (1.0 / (4 * pieces)) - product * (1.0 / (factor * STUDENT_TEMP))
            loss_ref[...] = loss + jnp.zeros((1, 128), F32)
            for copy in copies:
                copy.wait()

    out_shape = [hbm((half, steps * width), F32)] * 2
    out_specs = [pl.BlockSpec((half, width), lambda i, s: (0, i))] * 2
    operands = [protos, mass, column_sums, row_sum, rows, cols, offsets]
    in_specs = [
        pl.BlockSpec((dim, width), lambda i, s: (0, s[0] * total_steps + s[3] + i)),
    ] + [WHOLE] * 6
    aliases = {}
    scratch = []
    if last:
        operands.append(norm_sum)
        in_specs.append(WHOLE)
    if not first:
        operands += list(carried)
        in_specs += [WHOLE] * 2
    if last:
        shape = (pieces, crops, piece_images, dim)
        out_shape = out_shape + [hbm(shape, F32)] * 4 + [jax.ShapeDtypeStruct((1, 128), F32)]
        out_specs = out_specs + [pl.BlockSpec(memory_space=pl.ANY)] * 4 + [WHOLE]
    else:
        out_shape = out_shape + [vmem((groups, crops, images, dim), F32), vmem((teacher_rows, dim), F32)]
        out_specs = out_specs + [WHOLE] * 2
        if not first:
            aliases = {8: 2, 9: 3}
    scratch += [
        pltpu.VMEM((row_count, width), BF16),
        pltpu.VMEM((teacher_rows, width), BF16),
        pltpu.VMEM((teacher_rows, 128), F32),
        pltpu.VMEM((dim, width), F32),
        pltpu.VMEM((part_rows, width), F32),
        pltpu.VMEM((part_rows, width), F32),
    ]
    if last:
        assert steps == 1 and not first
        scratch.append(pltpu.SemaphoreType.DMA((4 * pieces,)))
    return pl.pallas_call(
        kernel,
        grid_spec=pltpu.PrefetchScalarGridSpec(
            num_scalar_prefetch=1, grid=(steps,), in_specs=in_specs, out_specs=out_specs, scratch_shapes=scratch
        ),
        out_shape=out_shape,
        input_output_aliases=aliases,
        compiler_params=params(),
        cost_estimate=cost(10),
        name="gradients",
    )(place, *operands)


def assemble(place, pieces, first, base):
    rows = pieces[0][0].shape[0]
    count = 4 * len(pieces)
    quarter = sum(CHUNKS)
    unit = pieces[0][0].shape[1] // CHUNKS[first]
    columns = 4 * quarter * unit
    flat = [piece for chunk in pieces for piece in chunk]

    def kernel(place_ref, *refs):
        out_ref, sem_ref = refs[-2:]
        copies = []
        for chunk in range(len(pieces)):
            width = CHUNKS[first + chunk] * unit
            offset = sum(CHUNKS[: first + chunk]) * unit
            for j in range(4):
                at = pl.multiple_of((place_ref[0] ^ j) * (quarter * unit) + offset, 128)
                index = 4 * chunk + j
                copies.append(
                    pltpu.make_async_copy(refs[index], out_ref.at[:, pl.ds(at, width)], sem_ref.at[index])
                )
                copies[-1].start()
        for copy in copies:
            copy.wait()

    anywhere = pl.BlockSpec(memory_space=pl.ANY)
    operands = flat if base is None else flat + [base]
    return pl.pallas_call(
        kernel,
        in_specs=[SCALARS] + [anywhere] * len(operands),
        out_specs=anywhere,
        out_shape=jax.ShapeDtypeStruct((rows, columns), F32),
        scratch_shapes=[pltpu.SemaphoreType.DMA((count,))],
        input_output_aliases={} if base is None else {1 + count: 0},
        compiler_params=params(),
        cost_estimate=cost(1.5),
        name="assemble",
    )(place, *operands)


def finish(near, received, unit, raw):
    shape = near.shape
    rows = [value.reshape(-1, shape[-1]) for value in (near, received, unit, raw)]

    def kernel(near_ref, received_ref, unit_ref, raw_ref, out_ref):
        cotangent = near_ref[...] + received_ref[...]
        unit = unit_ref[...]
        floats = raw_ref[...].astype(F32)
        scale = lax.rsqrt(jnp.sum(floats * floats, axis=1, keepdims=True) + NORM_EPS)
        out_ref[...] = scale * (cotangent - unit * jnp.sum(unit * cotangent, axis=1, keepdims=True))

    return pl.pallas_call(
        kernel,
        in_specs=[WHOLE] * 4,
        out_specs=WHOLE,
        out_shape=jax.ShapeDtypeStruct(rows[0].shape, F32),
        compiler_params=params(),
        cost_estimate=cost(1),
        name="finish",
    )(*rows).reshape(shape)


def step_on_device(student_features, teacher_features, student_prototypes, teacher_prototypes):
    student_prototypes = pltpu.with_memory_space_constraint(student_prototypes, pltpu.HBM)
    teacher_prototypes = pltpu.with_memory_space_constraint(teacher_prototypes, pltpu.HBM)
    crops, images, dim = student_features.shape
    proto_local = student_prototypes.shape[1]
    batch_devices = lax.axis_size(BATCH)
    proto_devices = lax.axis_size(PROTO)
    batch_bits = bits_of(batch_devices)
    proto_bits = bits_of(proto_devices)
    images_all = images * batch_devices
    sample_number = teacher_features.shape[0] * images_all
    factor = 1.0 / (images_all * PAIRS * STUDENT_TEMP)
    batch_index = lax.axis_index(BATCH)
    proto_index = lax.axis_index(PROTO)
    core, top = 0, batch_bits - 1
    middle = list(range(1, top))
    place = ((batch_index >> top) & 1) * 2 + (batch_index & 1)
    own_images = images // proto_devices
    columns = proto_local // 4
    places = jnp.stack([place, batch_index, proto_index]).astype(jnp.int32)
    chunk_places = [
        jnp.stack([place, batch_index, proto_index, jnp.int32(sum(CHUNKS[:chunk]))]).astype(jnp.int32)
        for chunk in range(len(CHUNKS))
    ]
    row_places = jnp.stack([place, proto_index]).astype(jnp.int32)

    teacher_own = unit_values(teacher_features.reshape(-1, dim))
    teacher_core = swap(teacher_own, BATCH, core)
    teacher_far = swap(teacher_own, BATCH, top)
    teacher_far_core = swap(teacher_far, BATCH, core)

    own_rows = unit_values(student_features.reshape(-1, dim))
    all_sums = row_sums(places, own_rows, student_prototypes, min(1024, proto_local))

    mass, column_sum = teacher_mass(
        places,
        [teacher_own, teacher_core, teacher_far, teacher_far_core],
        teacher_prototypes,
        columns,
        min(1024, columns),
    )

    own_start = proto_index * own_images
    unit_own = lax.dynamic_slice_in_dim(own_rows.reshape(crops, images, dim), own_start, own_images, 1)
    raw_own = lax.dynamic_slice_in_dim(student_features, own_start, own_images, 1)
    far = swap(unit_own, BATCH, top)[None]
    for bit in range(proto_bits):
        received = swap(far, PROTO, bit)
        far = jnp.concatenate([far, received], axis=0)
    core_rows = swap(own_rows, BATCH, core)
    far_core = swap(far, BATCH, core)
    rows, cols = gather_rows(row_places, own_rows, core_rows, far, far_core, crops, images)

    row_parts = None
    for sweep_index in range(SK_ITERS):
        if sweep_index:
            column_sum = column_pass(row_parts, mass, sample_number)
        for bit in middle[:-1]:
            column_sum = column_sum + swap(column_sum, BATCH, bit)
        column_parts = (column_sum, swap(column_sum, BATCH, middle[-1]))
        row_sum = row_pass(column_parts, mass, None if sweep_index else all_sums)
        row_sum = bits_sum(row_sum, PROTO, range(proto_bits))
        received = swap(row_sum, BATCH, top)
        row_sum = row_sum + received
        row_parts = (row_sum, swap(row_sum, BATCH, core))
        if sweep_index == 0:
            offsets, norm_sum = row_offsets(row_parts, mass.shape[0], crops, images, factor)

    row_total = row_parts[0] + row_parts[1]
    column_total = column_parts[0] + column_parts[1]
    order = [0]
    for bit in [core, top] + middle[::-1]:
        order = order + [j | (1 << bit) for j in order]
    geometry = (crops, images, proto_devices, batch_devices, factor, order)
    carried = None
    pieces = []
    for chunk, steps in enumerate(CHUNKS):
        outs = gradients(
            chunk_places[chunk], steps, chunk == 0, chunk == len(CHUNKS) - 1, student_prototypes, mass,
            column_total, row_total, rows, cols, offsets, norm_sum, carried, geometry,
        )
        send, keep = outs[:2]
        carried = outs[2:]
        for bit in middle[:-1]:
            keep = keep + swap(send, BATCH, bit)
            end = keep.shape[0]
            send = keep[end // 2 :]
            keep = keep[: end // 2]
        half = keep.shape[0] // 2
        quarter = half // 2
        received = swap(send, BATCH, middle[-1])
        far_send = keep[half:] + received[half:]
        near_own = keep[:quarter] + received[:quarter]
        near_core = keep[quarter:half] + received[quarter:half]
        far_half = swap(far_send, BATCH, top)
        near_core = swap(near_core, BATCH, core)
        far_core = far_half[quarter:half]
        far_core = swap(far_core, BATCH, core)
        pieces.append([near_own, near_core, far_half[:quarter], far_core])
    early = len(CHUNKS) - 2
    grad_prototypes = assemble(places, pieces[:early], 0, None)
    grad_prototypes = assemble(places, pieces[early:], early, grad_prototypes)

    far_wings, near_wings, loss = carried[:2], carried[2:4], carried[4]
    received = [swap(far_wings[1], BATCH, core)]
    received = [swap(far_wings[0], BATCH, core)] + received
    totals = []
    for wing in range(2):
        part = (near_wings[wing] + received[wing]).reshape((2,) * proto_bits + (crops, own_images, dim))
        axes = list(range(proto_bits))
        axes = axes[wing % proto_bits :] + axes[: wing % proto_bits]
        for axis in axes:
            bit = proto_bits - 1 - axis
            near = lax.slice_in_dim(part, 0, 1, axis=axis)
            away = lax.slice_in_dim(part, 1, 2, axis=axis)
            part = near + swap(away, PROTO, bit)
        totals.append(part.reshape(crops, own_images, dim))
    received = swap(totals[1], BATCH, top)
    grad_features = finish(totals[0], received, unit_own, raw_own)

    received = swap(loss, BATCH, core)
    loss = bits_sum(loss + received, BATCH, range(1, batch_bits))
    loss = bits_sum(loss, PROTO, range(proto_bits))
    mean_loss = loss[0, 0] / (images_all * PAIRS)
    return (mean_loss, grad_features, grad_prototypes)


def solution(mesh):
    placed = (P(None, BATCH, None), P(None, BATCH, None), P(None, PROTO), P(None, PROTO))
    return jax.shard_map(
        step_on_device,
        mesh=mesh,
        in_specs=placed,
        out_specs=(P(), P(None, (BATCH, PROTO), None), P(BATCH, PROTO)),
        check_vma=False,
    )
```

```python
import math

import jax
import jax.numpy as jnp
from jax import lax
from jax.experimental import pallas as pl
from jax.experimental.pallas import tpu as pltpu
from jax.sharding import PartitionSpec as P


CLUSTER_NUMBER = 65536
SK_ITERS = 3
BATCH = "batch"
PROTO = "proto"
PAIRS = 18

STUDENT_TEMP = 0.1
TEACHER_TEMP = 0.07
NORM_EPS = 1e-06
LOG2E = math.log2(math.e)

CHUNKS = (1, 2, 2, 2, 1)
MIB = 1 << 20
F32 = jnp.float32
BF16 = jnp.bfloat16
WHOLE = pl.BlockSpec(memory_space=pltpu.VMEM)
SCALARS = pl.BlockSpec(memory_space=pltpu.SMEM)


def vmem(shape, dtype):
    return pltpu.VMEM(shape, dtype)


def hbm(shape, dtype):
    return pltpu.HBM(shape, dtype)


def params():
    return pltpu.CompilerParams(vmem_limit_bytes=16 * MIB)


def cost(micros):
    return pl.CostEstimate(flops=int(micros * 1e9), transcendentals=0, bytes_accessed=int(micros * 1e6))


def exchange(value, axis, mask):
    size = lax.axis_size(axis)
    return lax.ppermute(value, axis, [(i, i ^ mask) for i in range(size)])


def swap(value, axis, bit):
    return exchange(value, axis, 1 << bit)


def bits_sum(value, axis, bits):
    for first in range(0, len(bits), 2):
        masks = [0]
        for bit in bits[first : first + 2]:
            masks += [mask | (1 << bit) for mask in masks]
        received = []
        for mask in masks[1:]:
            received.append(exchange(value, axis, mask))
        for part in received:
            value = value + part
    return value


def bits_of(size):
    return size.bit_length() - 1


def unit_values(values):
    def kernel(in_ref, out_ref):
        floats = in_ref[...].astype(F32)
        out_ref[...] = floats * lax.rsqrt(jnp.sum(floats * floats, axis=1, keepdims=True) + NORM_EPS)

    return pl.pallas_call(
        kernel,
        in_specs=[WHOLE],
        out_specs=WHOLE,
        out_shape=jax.ShapeDtypeStruct(values.shape, F32),
        compiler_params=params(),
        cost_estimate=cost(1),
        name="units",
    )(values)


def column_scale(floats):
    return lax.rsqrt(jnp.sum(floats * floats, axis=0, keepdims=True) + NORM_EPS)


def rows_to_lanes(partial):
    return jnp.concatenate(
        [
            jnp.sum(partial[i : i + 128].T, axis=0, keepdims=True)
            for i in range(0, partial.shape[0], 128)
        ],
        axis=1,
    )


def lanes_to_rows(values, start):
    return jnp.broadcast_to(values[:, start : start + 128], (128, 128)).T


def row_sums(place, unit, protos, width):
    rows, dim = unit.shape
    columns = protos.shape[1]
    steps = columns // width

    def kernel(place_ref, unit_ref, proto_ref, out_ref, rows_ref, sum_ref):
        step = pl.program_id(0)

        @pl.when(step == 0)
        def _():
            rows_ref[...] = unit_ref[...].astype(BF16)
            sum_ref[...] = jnp.zeros_like(sum_ref)

        for start in range(0, width, 512):
            floats = proto_ref[:, start : start + 512].astype(F32)
            proto_bf = (floats * column_scale(floats)).astype(BF16)
            cos = jnp.dot(rows_ref[...], proto_bf, preferred_element_type=F32)
            mass = jnp.exp2(cos * (LOG2E / STUDENT_TEMP))
            total = mass[:, :128]
            for lane in range(128, 512, 128):
                total = total + mass[:, lane : lane + 128]
            sum_ref[...] += total

        @pl.when(step == steps - 1)
        def _():
            out_ref[...] = jnp.zeros_like(out_ref)
            start = pl.multiple_of(place_ref[0] * rows, rows)
            out_ref[:, pl.ds(start, rows)] = rows_to_lanes(sum_ref[...])

    return pl.pallas_call(
        kernel,
        grid=(steps,),
        in_specs=[
            SCALARS,
            pl.BlockSpec((rows, dim), lambda i: (0, 0)),
            pl.BlockSpec((dim, width), lambda i: (0, i)),
        ],
        out_specs=pl.BlockSpec((1, 4 * rows), lambda i: (0, 0)),
        out_shape=jax.ShapeDtypeStruct((1, 4 * rows), F32),
        scratch_shapes=[pltpu.VMEM((rows, dim), BF16), pltpu.VMEM((rows, 128), F32)],
        compiler_params=params(),
        cost_estimate=cost(15),
        name="row_sums",
    )(place, unit, protos)


def teacher_mass(place, gathered, protos, columns, width):
    part_rows, dim = gathered[0].shape
    rows = part_rows * len(gathered)
    steps = columns // width

    def kernel(place_ref, *refs):
        parts = refs[: len(gathered)]
        proto_ref, mass_ref, sum_ref, rows_ref, parts_ref, sem_ref = refs[len(gathered) :]
        step = pl.program_id(0)

        @pl.when(step == 0)
        def _():
            copies = [
                pltpu.make_async_copy(part, parts_ref.at[j], sem_ref.at[j]) for j, part in enumerate(parts)
            ]
            for copy in copies:
                copy.start()
            for j, copy in enumerate(copies):
                copy.wait()
                start = pl.multiple_of((place_ref[0] ^ j) * part_rows, part_rows)
                rows_ref[pl.ds(start, part_rows)] = parts_ref[j].astype(BF16)

        at = pl.multiple_of(step * width, width)
        part = min(512, width)
        for start in range(0, width, part):
            floats = proto_ref[:, start : start + part].astype(F32)
            proto_bf = (floats * column_scale(floats)).astype(BF16)
            cos = jnp.dot(rows_ref[...], proto_bf, preferred_element_type=F32)
            mass = jnp.exp2(cos * (LOG2E / TEACHER_TEMP))
            mass_ref[:, pl.ds(at + start, part)] = mass
            sum_ref[:, start : start + part] = jnp.sum(mass, axis=0, keepdims=True)

    return pl.pallas_call(
        kernel,
        grid_spec=pltpu.PrefetchScalarGridSpec(
            num_scalar_prefetch=1,
            grid=(steps,),
            in_specs=[pl.BlockSpec(memory_space=pl.ANY)] * len(gathered)
            + [pl.BlockSpec((dim, width), lambda i, s: (0, s[0] * steps + i))],
            out_specs=[WHOLE, pl.BlockSpec((1, width), lambda i, s: (0, i))],
            scratch_shapes=[
                pltpu.VMEM((rows, dim), BF16),
                pltpu.VMEM((len(gathered), part_rows, dim), F32),
                pltpu.SemaphoreType.DMA((len(gathered),)),
            ],
        ),
        out_shape=[vmem((rows, columns), F32), jax.ShapeDtypeStruct((1, columns), F32)],
        compiler_params=params(),
        cost_estimate=cost(5),
        name="teacher_mass",
    )(place, *gathered, protos)


def row_pass(column_parts, mass, extra):
    rows, columns = mass.shape
    extras = [] if extra is None else [extra]
    total_rows = rows + sum(part.shape[1] for part in extras)

    def kernel(a_ref, b_ref, mass_ref, *refs):
        out_ref = refs[-1]
        scale = 1.0 / (CLUSTER_NUMBER * (a_ref[...] + b_ref[...]))

        def block(index, carry):
            start = pl.multiple_of(index * 128, 128)
            total = jnp.zeros((128, 128), F32)
            for lane in range(0, columns, 128):
                total = total + (
                    mass_ref[pl.ds(start, 128), lane : lane + 128] * scale[:, lane : lane + 128]
                )
            out_ref[:, pl.ds(start, 128)] = jnp.sum(total.T, axis=0, keepdims=True)
            return carry

        lax.fori_loop(0, rows // 128, block, 0, unroll=2)
        if extras:
            out_ref[:, rows:] = refs[0][...]

    return pl.pallas_call(
        kernel,
        in_specs=[WHOLE] * (3 + len(extras)),
        out_specs=WHOLE,
        out_shape=jax.ShapeDtypeStruct((1, total_rows), F32),
        compiler_params=params(),
        cost_estimate=cost(1.5),
        name="row_pass",
    )(*column_parts, mass, *extras)


def column_pass(row_parts, mass, sample_number):
    rows, columns = mass.shape

    def kernel(a_ref, b_ref, mass_ref, out_ref, scale_ref):
        scale = 1.0 / (sample_number * (a_ref[:, :rows] + b_ref[:, :rows]))
        for start in range(0, rows, 128):
            scale_ref[start : start + 128] = lanes_to_rows(scale, start)

        def block(index, carry):
            lane = pl.multiple_of(index * 256, 256)
            total = jnp.zeros((8, 256), F32)
            for start in range(0, rows, 128):
                scales = jnp.concatenate([scale_ref[start : start + 128]] * 2, axis=1)
                term = mass_ref[start : start + 128, pl.ds(lane, 256)] * scales
                total = total + jnp.sum(term.reshape(16, 8, 256), axis=0)
            out_ref[:, pl.ds(lane, 256)] = jnp.sum(total, axis=0, keepdims=True)
            return carry

        lax.fori_loop(0, columns // 256, block, 0, unroll=2)

    return pl.pallas_call(
        kernel,
        in_specs=[WHOLE] * 3,
        out_specs=WHOLE,
        out_shape=jax.ShapeDtypeStruct((1, columns), F32),
        scratch_shapes=[pltpu.VMEM((rows, 128), F32)],
        compiler_params=params(),
        cost_estimate=cost(1.5),
        name="column_pass",
    )(*row_parts, mass)


def gather_rows(place, own, core, far, far_core, crops, images):
    dim = own.shape[1]
    part_rows = crops * images
    pieces, _, piece_images, _ = far.shape
    rows = 4 * part_rows

    def kernel(place_ref, own_ref, core_ref, far_ref, far_core_ref, rows_ref, cols_ref, work_ref):
        def store(j, values):
            start = pl.multiple_of((place_ref[0] ^ j) * part_rows, part_rows)
            rows_ref[pl.ds(start, part_rows)] = values.astype(BF16)
            cols_ref[:, pl.ds(start, part_rows)] = values.T.astype(BF16)

        store(0, own_ref[...])
        store(1, core_ref[...])
        for j, ref in ((2, far_ref), (3, far_core_ref)):

            def move(crop, carry, ref=ref):
                for piece in range(pieces):
                    offset = (place_ref[1] ^ piece) * piece_images
                    at = pl.multiple_of(crop * images + offset, piece_images)
                    work_ref[pl.ds(at, piece_images)] = ref[piece, crop]
                return carry

            lax.fori_loop(0, crops, move, 0)
            store(j, work_ref[...])

    return pl.pallas_call(
        kernel,
        in_specs=[SCALARS] + [WHOLE] * 4,
        out_specs=[WHOLE] * 2,
        out_shape=[vmem((rows, dim), BF16), vmem((dim, rows), BF16)],
        scratch_shapes=[pltpu.VMEM((part_rows, dim), F32)],
        compiler_params=params(),
        cost_estimate=cost(3),
        name="gather_rows",
    )(place, own, core, far, far_core)


def row_offsets(parts, skip, crops, images, factor):
    rows = parts[0].shape[1] - skip

    def kernel(a_ref, b_ref, out_ref, norm_ref, sums_ref):
        sums_ref[...] = a_ref[:, skip:] + b_ref[:, skip:]

        def block(index, total):
            start = pl.multiple_of(index * 128, 128)
            pair_count = jnp.where((start // images) % crops < 2, F32(1.0), F32(2.0))
            sums = sums_ref[:, pl.ds(start, 128)]
            out_ref[pl.ds(start, 128)] = lanes_to_rows(jnp.log2((pair_count * factor) / sums), 0)
            return total + pair_count * jnp.log(sums)

        total = lax.fori_loop(0, rows // 128, block, jnp.zeros((1, 128), F32), unroll=10)
        norm_ref[...] = jnp.sum(total, axis=1, keepdims=True) + jnp.zeros((1, 128), F32)

    return pl.pallas_call(
        kernel,
        in_specs=[WHOLE] * 2,
        out_specs=[WHOLE] * 2,
        out_shape=[vmem((rows, 128), F32), jax.ShapeDtypeStruct((1, 128), F32)],
        scratch_shapes=[pltpu.VMEM((1, rows), F32)],
        compiler_params=params(),
        cost_estimate=cost(1),
        name="row_offsets",
    )(*parts)


def gradients(place, steps, first, last, protos, mass, column_sums, row_sum, rows, cols, offsets, norm_sum, carried, geometry):
    crops, images, pieces, blocks, factor, order = geometry
    dim = protos.shape[0]
    half = dim // 2
    row_count = rows.shape[0]
    teacher_rows, columns = mass.shape
    groups = teacher_rows // (2 * images)
    part_rows = crops * images
    piece_images = images // pieces
    total_steps = sum(CHUNKS)
    width = columns // total_steps
    block_rows = dim // blocks

    def kernel(place_ref, *refs):
        refs = list(refs)
        proto_ref, mass_ref, csum_ref, rsum_ref, rows_ref, cols_ref, offs_ref = refs[:7]
        refs = refs[7:]
        if last:
            norm_ref = refs.pop(0)
        if not first:
            feat_in, targ_in = refs[:2]
            refs = refs[2:]
        send_ref, keep_ref = refs[:2]
        refs = refs[2:]
        if last:
            wing_refs, loss_ref = refs[:4], refs[4]
            refs = refs[5:]
            sem_ref = refs.pop()
            feat_ref, targ_ref = feat_in, targ_in
        else:
            feat_ref, targ_ref = refs[:2]
            refs = refs[2:]
        grad_ref, tbf_ref, rscale_ref, weight_ref, *cos_refs = refs
        step = pl.program_id(0)

        @pl.when(step == 0)
        def _():
            scale = factor / rsum_ref[...]
            for start in range(0, teacher_rows, 128):
                rscale_ref[start : start + 128] = lanes_to_rows(scale, start)
            if first:

                def clear(crop, carry):
                    feat_ref[:, pl.ds(crop, 1)] = jnp.zeros((groups, 1, images, dim), F32)
                    return carry

                lax.fori_loop(0, crops, clear, 0)
                targ_ref[...] = jnp.zeros_like(targ_ref)

        at = pl.multiple_of((place_ref[3] + step) * width, width)
        floats = proto_ref[...].astype(F32)
        inverse = column_scale(floats)
        unit = floats * inverse
        proto_bf = unit.astype(BF16)
        proto_t = unit.T.astype(BF16)
        cscale = 1.0 / (CLUSTER_NUMBER * csum_ref[:, pl.ds(at, width)])

        for group in range(groups):
            base = group * part_rows
            tbase = group * 2 * images
            cos_ref = cos_refs[group % 2]
            cos_ref[...] = jnp.dot(rows_ref[base : base + part_rows], proto_bf, preferred_element_type=F32)
            for lane in range(0, width, 128):
                lanes = slice(lane, lane + 128)
                for image in range(0, images, 64):
                    pair = []
                    for wide in range(2):
                        start = tbase + wide * images + image
                        target = (
                            mass_ref[start : start + 64, pl.ds(at + lane, 128)]
                            * rscale_ref[start : start + 64]
                            * cscale[:, lanes]
                        )
                        tbf_ref[start : start + 64, lanes] = target.astype(BF16)
                        pair.append(target)
                    both = pair[0] + pair[1]
                    for crop in range(crops):
                        start = crop * images + image
                        power = cos_ref[start : start + 64, lanes] * (LOG2E / STUDENT_TEMP)
                        prob = jnp.exp2(power + offs_ref[base + start : base + start + 64])
                        target = pair[1] if crop == 0 else pair[0] if crop == 1 else both
                        grad_ref[base + start : base + start + 64, lanes] = (prob - target).astype(BF16)
            product = jnp.dot(grad_ref[base : base + part_rows], proto_t, preferred_element_type=F32)
            feat_ref[group] += product.reshape(crops, images, dim)
        copies = []
        if last:
            for j in range(4):
                dest = wing_refs[(j >> 1) + (0 if j & 1 else 2)]
                for piece in range(pieces):
                    start = pl.multiple_of((place_ref[2] ^ piece) * piece_images, piece_images)
                    copies.append(
                        pltpu.make_async_copy(
                            feat_ref.at[place_ref[0] ^ j, :, pl.ds(start, piece_images)],
                            dest.at[piece],
                            sem_ref.at[len(copies)],
                        )
                    )
                    copies[-1].start()
        targ_ref[...] += jnp.dot(tbf_ref[...], proto_t, preferred_element_type=F32)
        weight_ref[...] = jnp.zeros_like(weight_ref)

        def part_of_rows(index, carry):
            part = pl.ds(pl.multiple_of(index * (row_count // 2), row_count // 2), row_count // 2)
            weight_ref[...] += jnp.dot(cols_ref[:, part], grad_ref[part], preferred_element_type=F32)
            return carry

        lax.fori_loop(0, 2, part_of_rows, 0)
        weight = weight_ref[...]
        curvature = jnp.sum(proto_bf.astype(F32) * weight, axis=0, keepdims=True)
        weight_ref[...] = inverse * (weight - unit * curvature)
        for position, j in enumerate(order):
            start = pl.multiple_of((place_ref[1] ^ j) * block_rows, block_rows)
            dest, index = (keep_ref, position) if position < blocks // 2 else (send_ref, position - blocks // 2)
            dest[index * block_rows : (index + 1) * block_rows] = weight_ref[pl.ds(start, block_rows)]

        if last:
            total = jnp.zeros((images, dim), F32)
            for group in range(groups):
                base = group * part_rows
                tbase = group * 2 * images
                crop_rows = [
                    rows_ref[base + c * images : base + (c + 1) * images].astype(F32) for c in range(crops)
                ]
                shared = crop_rows[2]
                for c in range(3, crops):
                    shared = shared + crop_rows[c]
                total = total + targ_ref[tbase : tbase + images] * (crop_rows[1] + shared)
                total = total + targ_ref[tbase + images : tbase + 2 * images] * (crop_rows[0] + shared)
            product = jnp.sum(jnp.sum(total, axis=0, keepdims=True), axis=1, keepdims=True)
            loss = norm_ref[:, :1] * (1.0 / (4 * pieces)) - product * (1.0 / (factor * STUDENT_TEMP))
            loss_ref[...] = loss + jnp.zeros((1, 128), F32)
            for copy in copies:
                copy.wait()

    out_shape = [hbm((half, steps * width), F32)] * 2
    out_specs = [pl.BlockSpec((half, width), lambda i, s: (0, i))] * 2
    operands = [protos, mass, column_sums, row_sum, rows, cols, offsets]
    in_specs = [
        pl.BlockSpec((dim, width), lambda i, s: (0, s[0] * total_steps + s[3] + i)),
    ] + [WHOLE] * 6
    aliases = {}
    scratch = []
    if last:
        operands.append(norm_sum)
        in_specs.append(WHOLE)
    if not first:
        operands += list(carried)
        in_specs += [WHOLE] * 2
    if last:
        shape = (pieces, crops, piece_images, dim)
        out_shape = out_shape + [hbm(shape, F32)] * 4 + [jax.ShapeDtypeStruct((1, 128), F32)]
        out_specs = out_specs + [pl.BlockSpec(memory_space=pl.ANY)] * 4 + [WHOLE]
    else:
        out_shape = out_shape + [vmem((groups, crops, images, dim), F32), vmem((teacher_rows, dim), F32)]
        out_specs = out_specs + [WHOLE] * 2
        if not first:
            aliases = {8: 2, 9: 3}
    scratch += [
        pltpu.VMEM((row_count, width), BF16),
        pltpu.VMEM((teacher_rows, width), BF16),
        pltpu.VMEM((teacher_rows, 128), F32),
        pltpu.VMEM((dim, width), F32),
        pltpu.VMEM((part_rows, width), F32),
        pltpu.VMEM((part_rows, width), F32),
    ]
    if last:
        assert steps == 1 and not first
        scratch.append(pltpu.SemaphoreType.DMA((4 * pieces,)))
    return pl.pallas_call(
        kernel,
        grid_spec=pltpu.PrefetchScalarGridSpec(
            num_scalar_prefetch=1, grid=(steps,), in_specs=in_specs, out_specs=out_specs, scratch_shapes=scratch
        ),
        out_shape=out_shape,
        input_output_aliases=aliases,
        compiler_params=params(),
        cost_estimate=cost(10),
        name="gradients",
    )(place, *operands)


def assemble(place, pieces, first, base):
    rows = pieces[0][0].shape[0]
    count = 4 * len(pieces)
    quarter = sum(CHUNKS)
    unit = pieces[0][0].shape[1] // CHUNKS[first]
    columns = 4 * quarter * unit
    flat = [piece for chunk in pieces for piece in chunk]

    def kernel(place_ref, *refs):
        out_ref, sem_ref = refs[-2:]
        copies = []
        for chunk in range(len(pieces)):
            width = CHUNKS[first + chunk] * unit
            offset = sum(CHUNKS[: first + chunk]) * unit
            for j in range(4):
                at = pl.multiple_of((place_ref[0] ^ j) * (quarter * unit) + offset, 128)
                index = 4 * chunk + j
                copies.append(
                    pltpu.make_async_copy(refs[index], out_ref.at[:, pl.ds(at, width)], sem_ref.at[index])
                )
                copies[-1].start()
        for copy in copies:
            copy.wait()

    anywhere = pl.BlockSpec(memory_space=pl.ANY)
    operands = flat if base is None else flat + [base]
    return pl.pallas_call(
        kernel,
        in_specs=[SCALARS] + [anywhere] * len(operands),
        out_specs=anywhere,
        out_shape=jax.ShapeDtypeStruct((rows, columns), F32),
        scratch_shapes=[pltpu.SemaphoreType.DMA((count,))],
        input_output_aliases={} if base is None else {1 + count: 0},
        compiler_params=params(),
        cost_estimate=cost(1.5),
        name="assemble",
    )(place, *operands)


def finish(near, received, unit, raw):
    shape = near.shape
    rows = [value.reshape(-1, shape[-1]) for value in (near, received, unit, raw)]

    def kernel(near_ref, received_ref, unit_ref, raw_ref, out_ref):
        cotangent = near_ref[...] + received_ref[...]
        unit = unit_ref[...]
        floats = raw_ref[...].astype(F32)
        scale = lax.rsqrt(jnp.sum(floats * floats, axis=1, keepdims=True) + NORM_EPS)
        out_ref[...] = scale * (cotangent - unit * jnp.sum(unit * cotangent, axis=1, keepdims=True))

    return pl.pallas_call(
        kernel,
        in_specs=[WHOLE] * 4,
        out_specs=WHOLE,
        out_shape=jax.ShapeDtypeStruct(rows[0].shape, F32),
        compiler_params=params(),
        cost_estimate=cost(1),
        name="finish",
    )(*rows).reshape(shape)


def step_on_device(student_features, teacher_features, student_prototypes, teacher_prototypes):
    student_prototypes = pltpu.with_memory_space_constraint(student_prototypes, pltpu.HBM)
    teacher_prototypes = pltpu.with_memory_space_constraint(teacher_prototypes, pltpu.HBM)
    crops, images, dim = student_features.shape
    proto_local = student_prototypes.shape[1]
    batch_devices = lax.axis_size(BATCH)
    proto_devices = lax.axis_size(PROTO)
    batch_bits = bits_of(batch_devices)
    proto_bits = bits_of(proto_devices)
    images_all = images * batch_devices
    sample_number = teacher_features.shape[0] * images_all
    factor = 1.0 / (images_all * PAIRS * STUDENT_TEMP)
    batch_index = lax.axis_index(BATCH)
    proto_index = lax.axis_index(PROTO)
    core, top = 0, batch_bits - 1
    middle = list(range(1, top))
    place = ((batch_index >> top) & 1) * 2 + (batch_index & 1)
    own_images = images // proto_devices
    columns = proto_local // 4
    places = jnp.stack([place, batch_index, proto_index]).astype(jnp.int32)
    chunk_places = [
        jnp.stack([place, batch_index, proto_index, jnp.int32(sum(CHUNKS[:chunk]))]).astype(jnp.int32)
        for chunk in range(len(CHUNKS))
    ]
    row_places = jnp.stack([place, proto_index]).astype(jnp.int32)

    teacher_own = unit_values(teacher_features.reshape(-1, dim))
    teacher_core = swap(teacher_own, BATCH, core)
    teacher_far = swap(teacher_own, BATCH, top)
    teacher_far_core = swap(teacher_far, BATCH, core)

    own_rows = unit_values(student_features.reshape(-1, dim))
    all_sums = row_sums(places, own_rows, student_prototypes, min(1024, proto_local))

    mass, column_sum = teacher_mass(
        places,
        [
            pltpu.with_memory_space_constraint(part, pltpu.HBM)
            for part in (teacher_own, teacher_core, teacher_far, teacher_far_core)
        ],
        teacher_prototypes,
        columns,
        min(1024, columns),
    )

    own_start = proto_index * own_images
    unit_own = lax.dynamic_slice_in_dim(own_rows.reshape(crops, images, dim), own_start, own_images, 1)
    raw_own = lax.dynamic_slice_in_dim(student_features, own_start, own_images, 1)
    far = swap(unit_own, BATCH, top)[None]
    for bit in range(proto_bits):
        received = swap(far, PROTO, bit)
        far = jnp.concatenate([far, received], axis=0)
    core_rows = swap(own_rows, BATCH, core)
    far_core = swap(far, BATCH, core)
    rows, cols = gather_rows(row_places, own_rows, core_rows, far, far_core, crops, images)

    row_parts = None
    for sweep_index in range(SK_ITERS):
        if sweep_index:
            column_sum = column_pass(row_parts, mass, sample_number)
        for bit in middle[:-1]:
            column_sum = column_sum + swap(column_sum, BATCH, bit)
        column_parts = (column_sum, swap(column_sum, BATCH, middle[-1]))
        row_sum = row_pass(column_parts, mass, None if sweep_index else all_sums)
        row_sum = bits_sum(row_sum, PROTO, range(proto_bits))
        received = swap(row_sum, BATCH, top)
        row_sum = row_sum + received
        row_parts = (row_sum, swap(row_sum, BATCH, core))
        if sweep_index == 0:
            offsets, norm_sum = row_offsets(row_parts, mass.shape[0], crops, images, factor)

    row_total = row_parts[0] + row_parts[1]
    column_total = column_parts[0] + column_parts[1]
    order = [0]
    for bit in [core, top] + middle[::-1]:
        order = order + [j | (1 << bit) for j in order]
    geometry = (crops, images, proto_devices, batch_devices, factor, order)
    carried = None
    pieces = []
    for chunk, steps in enumerate(CHUNKS):
        outs = gradients(
            chunk_places[chunk], steps, chunk == 0, chunk == len(CHUNKS) - 1, student_prototypes, mass,
            column_total, row_total, rows, cols, offsets, norm_sum, carried, geometry,
        )
        send, keep = outs[:2]
        carried = outs[2:]
        for bit in middle[:-1]:
            keep = keep + swap(send, BATCH, bit)
            end = keep.shape[0]
            send = keep[end // 2 :]
            keep = keep[: end // 2]
        half = keep.shape[0] // 2
        quarter = half // 2
        received = swap(send, BATCH, middle[-1])
        far_send = keep[half:] + received[half:]
        near_own = keep[:quarter] + received[:quarter]
        near_core = keep[quarter:half] + received[quarter:half]
        far_half = swap(far_send, BATCH, top)
        near_core = swap(near_core, BATCH, core)
        far_core = far_half[quarter:half]
        far_core = swap(far_core, BATCH, core)
        pieces.append([near_own, near_core, far_half[:quarter], far_core])
    early = len(CHUNKS) - 2
    grad_prototypes = assemble(places, pieces[:early], 0, None)
    grad_prototypes = assemble(places, pieces[early:], early, grad_prototypes)

    far_wings, near_wings, loss = carried[:2], carried[2:4], carried[4]
    received = [swap(far_wings[1], BATCH, core)]
    received = [swap(far_wings[0], BATCH, core)] + received
    totals = []
    for wing in range(2):
        part = (near_wings[wing] + received[wing]).reshape((2,) * proto_bits + (crops, own_images, dim))
        axes = list(range(proto_bits))
        axes = axes[wing % proto_bits :] + axes[: wing % proto_bits]
        for axis in axes:
            bit = proto_bits - 1 - axis
            near = lax.slice_in_dim(part, 0, 1, axis=axis)
            away = lax.slice_in_dim(part, 1, 2, axis=axis)
            part = near + swap(away, PROTO, bit)
        totals.append(part.reshape(crops, own_images, dim))
    received = swap(totals[1], BATCH, top)
    grad_features = finish(totals[0], received, unit_own, raw_own)

    received = swap(loss, BATCH, core)
    loss = bits_sum(loss + received, BATCH, range(1, batch_bits))
    loss = bits_sum(loss, PROTO, range(proto_bits))
    mean_loss = loss[0, 0] / (images_all * PAIRS)
    return (mean_loss, grad_features, grad_prototypes)


def solution(mesh):
    placed = (P(None, BATCH, None), P(None, BATCH, None), P(None, PROTO), P(None, PROTO))
    return jax.shard_map(
        step_on_device,
        mesh=mesh,
        in_specs=placed,
        out_specs=(P(), P(None, (BATCH, PROTO), None), P(BATCH, PROTO)),
        check_vma=False,
    )
```
